128 devices in a mesh: tx: 16 (over y, x), ty: 8 (over z, core).
Axes of the slice: x: 4, y: 4, z: 4, core: 2. Of those that a mesh axis runs over, the one named last changes fastest.
Arguments:
- adjoint_in: float32 [50, 1024, 1024], P(None, 'tx', 'ty'), may hold values from -6 to 6
- state_theta: bfloat16 [50, 1024, 1024], P(None, 'tx', 'ty'), may hold values from -6 to 6
- state_u: bfloat16 [50, 1024, 1024], P(None, 'tx', 'ty'), may hold values from -1.796875 to 1.796875
- state_v: bfloat16 [50, 1024, 1024], P(None, 'tx', 'ty'), may hold values from -1.796875 to 1.796875
- level_scale: float32 [3, 50], replicated, may hold values from 0.5 to 2
- land_mask: int32 [1024, 1024], P('tx', 'ty'), may hold values 0 or 1
- level_weights: float32 [50], replicated, may hold values from 0.02 to 0.2
- column_weight: float32 [1024, 1024], P('tx', 'ty'), may hold values from 0.5 to 2
Outputs:
- adjoint_out: float32 [50, 1024, 1024], P(None, 'tx', 'ty')
- surface_adjoint: float32 [1024, 1024], P('tx', 'ty')
The draws below stay inside these ranges and needn't reach their ends.
All inputs are finite; a program needn't handle non-finite values. No bound on the sum of `land_mask` on one device may be relied on, other than what follows from the above.
Results may differ from the reference program's by a relative error of at most 0.0003.
Values may be sent and summed in bfloat16 or wider, within the bound.
No kernel may reach another device: no remote copies, remote signals or barrier semaphores. Data moves between devices by JAX's collectives and lax.ppermute only.
A program may use at most 192 MiB of HBM per device.

```python
import math
import jax
import jax.numpy as jnp

K = 50
ITERS = 12
NX = 1024
NY = 1024


def with_ends(drawn, stream_key, least, top_value):
    extent = drawn.shape
    index_at = [jax.random.randint(jax.random.fold_in(stream_key, axis), (), 0, extent[axis]) for axis in range(len(extent))]
    drawn = drawn.at[tuple(index_at)].set(least)
    longest = extent.index(max(extent))
    index_at[longest] = (index_at[longest] + 1) % extent[longest]
    return drawn.at[tuple(index_at)].set(top_value)


def levels(rng, dims, shards, low, high):
    def one(position, shards_of):
        draws = jax.random.uniform(jax.random.fold_in(jax.random.fold_in(rng, 6), position), (shards_of,), jnp.float32, low / len(shards), high / len(shards))
        return jnp.repeat(jnp.exp(draws), dims[position] // shards_of).reshape((-1,) + (1,) * (len(dims) - position - 1))

    gain = one(*shards[0])
    for cut in shards[1:]:
        gain = gain * one(*cut)
    return gain


def noise(rng, shape, width, limit, cuts=(), held_as=jnp.bfloat16):
    entries = jax.random.normal(rng, shape, jnp.float32) * width
    if len(cuts) > 0:
        entries = levels(rng, shape, cuts, -0.22, 0.18) * entries
    return jnp.clip(entries, min=-limit, max=limit).astype(held_as)


def setup_inputs(seed: int = 0) -> dict:
    arg_keys = jax.random.split(jax.random.key(seed), 9)
    return {
        "adjoint_in": noise(arg_keys[0], (K, NX, NY), 1.0, 6.0, ((1, 16), (2, 8)), jnp.float32),
        "state_theta": noise(arg_keys[1], (K, NX, NY), 1.0, 6.0, ((1, 16), (2, 8))),
        "state_u": noise(arg_keys[2], (K, NX, NY), 0.3, 1.796875, ((1, 16), (2, 8))),
        "state_v": noise(arg_keys[3], (K, NX, NY), 0.3, 1.796875, ((1, 16), (2, 8))),
        "level_scale": jnp.clip(jnp.exp(jax.random.uniform(arg_keys[4], (3, K), jnp.float32, math.log(0.5), math.log(2.0))), 0.5, 2.0),
        "land_mask": with_ends((jax.random.randint(arg_keys[5], (NX, NY), 0, 5) < 4).astype(jnp.int32), jax.random.fold_in(arg_keys[5], 1), 0, 1),
        "level_weights": jnp.clip(jnp.exp(jax.random.uniform(arg_keys[6], (K,), jnp.float32, math.log(0.02), math.log(0.2))), 0.02, 0.2),
        "column_weight": jnp.clip(jnp.exp(math.log(2.0) - 1.3862944 * jax.random.uniform(arg_keys[7], (NX, NY), jnp.float32) ** levels(arg_keys[7], (NX, NY), ((0, 16), (1, 8)), -0.2, 0.2)), 0.5, 2.0),
    }


def interior(p):
    return p[..., 1:-1, 1:-1]


def stepped_field(lam, theta, vel_u, vel_v, wet):
    kappa = 0.05 * (1.5 + jnp.tanh(theta))
    lc = interior(lam)
    le = lam[..., 2:, 1:-1]
    lw = lam[..., :-2, 1:-1]
    ln = lam[..., 1:-1, 2:]
    ls = lam[..., 1:-1, :-2]
    kc = interior(kappa)
    mc = interior(wet)
    m_east = mc * wet[2:, 1:-1]
    m_west = mc * wet[:-2, 1:-1]
    m_north = mc * wet[1:-1, 2:]
    m_south = mc * wet[1:-1, :-2]
    diffusion = 0.5 * (kc + kappa[..., 2:, 1:-1]) * m_east * (le - lc)
    diffusion = diffusion - 0.5 * (kc + kappa[..., :-2, 1:-1]) * m_west * (lc - lw)
    diffusion = diffusion + 0.5 * (kc + kappa[..., 1:-1, 2:]) * m_north * (ln - lc)
    diffusion = diffusion - 0.5 * (kc + kappa[..., 1:-1, :-2]) * m_south * (lc - ls)
    advection = m_east * interior(vel_u) * 0.5 * (le - lc) + m_west * vel_u[..., :-2, 1:-1] * 0.5 * (lc - lw)
    advection = advection + m_north * interior(vel_v) * 0.5 * (ln - lc) + m_south * vel_v[..., 1:-1, :-2] * 0.5 * (lc - ls)
    kface = 0.5 * (kc[1:] + kc[:-1])
    zflux = kface * (lc[1:] - lc[:-1])
    zeros = jnp.zeros_like(lc[:1])
    vertical = jnp.concatenate([zflux, zeros], 0) - jnp.concatenate([zeros, zflux], 0)
    return mc * (lc + diffusion + vertical + advection)


def surface_operator(padded, wet, column_weight):
    mc = interior(wet)
    sc = interior(padded)
    total = mc * wet[2:, 1:-1] * (sc - padded[2:, 1:-1])
    total = total + mc * wet[:-2, 1:-1] * (sc - padded[:-2, 1:-1])
    total = total + mc * wet[1:-1, 2:] * (sc - padded[1:-1, 2:])
    total = total + mc * wet[1:-1, :-2] * (sc - padded[1:-1, :-2])
    return column_weight * sc + 4.0 * total


def pad_two(field):
    return jnp.pad(field, ((0, 0), (1, 1), (1, 1)))


def reference(adjoint_in, state_theta, state_u, state_v, level_scale, land_mask, level_weights, column_weight):
    theta = state_theta.astype(jnp.float32) * level_scale[0][:, None, None]
    vel_u = state_u.astype(jnp.float32) * level_scale[1][:, None, None]
    vel_v = state_v.astype(jnp.float32) * level_scale[2][:, None, None]
    wet = jnp.pad(land_mask.astype(jnp.float32), 1)
    stepped = stepped_field(pad_two(adjoint_in), pad_two(theta), pad_two(vel_u), pad_two(vel_v), wet)
    rhs = jnp.sum(level_weights[:, None, None] * stepped, axis=0)
    surface = jnp.zeros_like(rhs)
    residual = rhs
    direction = rhs
    norm_now = jnp.sum(residual * residual)
    for step in range(ITERS):
        image = surface_operator(jnp.pad(direction, 1), wet, column_weight)
        alpha = norm_now / jnp.sum(direction * image)
        surface = surface + alpha * direction
        residual = residual - alpha * image
        norm_next = jnp.sum(residual * residual)
        direction = residual + (norm_next / norm_now) * direction
        norm_now = norm_next
    wet_inner = land_mask.astype(jnp.float32)
    adjoint_out = stepped - level_weights[:, None, None] * (wet_inner * surface)[None]
    return adjoint_out, surface
```

```python
import jax
import jax.numpy as jnp
from jax import lax
from jax.experimental import pallas as pl
from jax.experimental.pallas import tpu as pltpu
from jax.sharding import PartitionSpec as P

ITERS = 12
LEVELS = 50
LP = 56
NX, NY = 64, 128
LB = 10
HALO = 12
LOW, HIGH = 0.7, 31.0
MID, HALF = 0.5 * (HIGH + LOW), 0.5 * (HIGH - LOW)
GUARD = 1.0e5
F32 = jnp.float32


def lanes(shape):
    return lax.broadcasted_iota(jnp.int32, shape, len(shape) - 1)


def rows_of(shape):
    return lax.broadcasted_iota(jnp.int32, shape, len(shape) - 2)


def roll(x, shift, axis):
    return pltpu.roll(x, shift % x.shape[axis], axis)


def half_kappa(theta, scale):
    return 0.025 * (1.5 + jnp.tanh(theta.astype(F32) * scale))


def interior_kernel(
    scale, weight, lam, lam_next, theta, theta_next, vel_u, vel_v, mask, column,
    stepped, sent, edge_rows, rhs, coupled, weights_out, flux,
):
    step = pl.program_id(0)
    tile = (NX, NY)
    lane, row = lanes(tile), rows_of(tile)
    wet = mask[...].astype(F32)

    @pl.when(step == 0)
    def _():
        sent[...] = jnp.zeros_like(sent)
        edge_rows[...] = jnp.zeros_like(edge_rows)
        rhs[...] = jnp.zeros_like(rhs)
        flux[...] = jnp.zeros_like(flux)
        weights_out[...] = jnp.zeros_like(weights_out)
        coupled[...] = wet * column[...]

    face_x = jnp.where(row == NX - 1, 0.0, wet * roll(wet, -1, 0))
    face_y = jnp.where(lane == NY - 1, 0.0, wet * roll(wet, -1, 1))
    half = half_kappa(theta[0], scale[0, step * LB])
    below = flux[...]
    total = rhs[...]
    for kk in range(LB):
        k = step * LB + kk
        w = weight[k]
        here = lam[kk]
        if kk + 1 < LB:
            above = lam[kk + 1]
            half_above = half_kappa(theta[kk + 1], scale[0, k + 1])
        else:
            above = lam_next[0]
            half_above = half_kappa(theta_next[0], scale[0, jnp.minimum(k + 1, LEVELS - 1)])
        half_u = vel_u[kk].astype(F32) * (0.5 * scale[1, k])
        half_v = vel_v[kk].astype(F32) * (0.5 * scale[2, k])
        dx = face_x * (roll(here, -1, 0) - here)
        sx = half + roll(half, -1, 0)
        dy = face_y * (roll(here, -1, 1) - here)
        sy = half + roll(half, -1, 1)
        vertical = (half + half_above) * (above - here)
        value = here + dx * (sx + half_u) + roll(dx * (half_u - sx), 1, 0)
        value = value + dy * (sy + half_v) + roll(dy * (half_v - sy), 1, 1)
        value = wet * (value + (vertical - below))
        stepped[kk] = value
        total = total + w * value
        at = 16 + 2 * k
        pair = (lane == at) | (lane == at + 1)
        shift = at + 1
        sent[0:64] = jnp.where(pair, pltpu.roll(here, shift, 1), sent[0:64])
        sent[64:128] = jnp.where(pair, pltpu.roll(half, shift, 1), sent[64:128])
        sent[128:192] = jnp.where(lane == at, pltpu.roll(half_v, shift, 1), sent[128:192])
        edge_rows[0, pl.ds(k, 1), :] = here[NX - 1 :]
        edge_rows[1, pl.ds(k, 1), :] = half[NX - 1 :]
        edge_rows[2, pl.ds(k, 1), :] = half_u[NX - 1 :]
        edge_rows[3, pl.ds(k, 1), :] = here[:1]
        edge_rows[4, pl.ds(k, 1), :] = half[:1]
        weights_out[pl.ds(k, 1), :] = jnp.full((1, NY), w, F32)
        lane8 = lanes((8, NY))
        weights_out[LP : LP + 8, :] = jnp.where(
            (lane8 == at) | (lane8 == at + 1), w, weights_out[LP : LP + 8, :]
        )
        below, half = vertical, half_above
    flux[...] = below
    rhs[...] = total

    @pl.when(step == LEVELS // LB - 1)
    def _():
        rim = (lane < HALO) | (lane >= NY - HALO)
        sent[0:64] = jnp.where(rim, total, sent[0:64])
        sent[64:128] = jnp.where(rim, coupled[...], sent[64:128])
        lane_e = lanes((LP, NY))
        packed = jnp.where((lane_e < HALO) | (lane_e >= NY - HALO), edge_rows[0], 0.0)
        for m in range(1, 5):
            inside = (lane_e >= 24 * m - HALO) & (lane_e < 24 * m + HALO)
            packed = jnp.where(inside, roll(edge_rows[m], 24 * m, 1), packed)
        sent[192 : 192 + LP] = packed


def column_kernel(
    from_south, from_north, sent, edge_rows, rhs, coupled, weights,
    down, up, rhs_out, outer, correction,
):
    j = lax.axis_index("ty")
    has_south = jnp.where(j > 0, 1.0, 0.0)
    has_north = jnp.where(j < lax.axis_size("ty") - 1, 1.0, 0.0)
    tile = (NX, NY)
    lane = lanes(tile)
    even = (lane & 1) == 0
    first, last = lane < HALO, lane >= NY - HALO
    south_c = from_south[64:128] * has_south
    north_c = from_north[64:128] * has_north
    outer_c = jnp.where(first, north_c, jnp.where(last, south_c, 0.0))
    outer_r = jnp.where(
        first, from_north[0:64] * has_north, jnp.where(last, from_south[0:64] * has_south, 0.0)
    )
    own_c = coupled[...]
    wet = jnp.where(own_c > 0.0, 1.0, 0.0)
    outer_wet = jnp.where(outer_c > 0.0, 1.0, 0.0)
    mask = jnp.where(
        even, wet[:, NY - 1 :] * outer_wet[:, :1], wet[:, :1] * outer_wet[:, NY - 1 :]
    )
    lam = jnp.where(even, roll(from_north[0:64], -1, 1), roll(from_south[0:64], 1, 1))
    half = jnp.where(even, roll(from_north[64:128], -1, 1), roll(from_south[64:128], 1, 1))
    speed = jnp.where(even, sent[128:192], -roll(from_south[128:192], 1, 1))
    gradient = mask * (lam - sent[0:64])
    both = half + sent[64:128]
    levels = (lane >= 16) & (lane < 16 + 2 * LEVELS)
    mine = jnp.where(levels, gradient * (both + speed), 0.0)
    theirs = jnp.where(levels, gradient * (speed - both), 0.0)
    correction[...] = mine
    w = weights[LP : LP + 1, :]

    def total(values, which):
        return jnp.sum(jnp.where(which, w * values, 0.0), axis=1, keepdims=True)

    odd = jnp.logical_not(even)
    own = rhs[...]
    own = own + jnp.where(lane == NY - 1, total(mine, even), 0.0)
    own = own + jnp.where(lane == 0, total(mine, odd), 0.0)
    outer_r = outer_r + jnp.where(lane == 0, total(theirs, even), 0.0)
    outer_r = outer_r + jnp.where(lane == NY - 1, total(theirs, odd), 0.0)
    rhs_out[...] = own
    outer[0:64] = outer_r
    outer[64:128] = outer_c
    lane_e = lanes((LP, NY))
    north = (lane_e >= 0) & (lane_e < HALO)
    for m in range(1, 5):
        north = north | ((lane_e >= 24 * m) & (lane_e < 24 * m + HALO))
    levels_outer = jnp.where(north, from_north[192 : 192 + LP], from_south[192 : 192 + LP])
    strip_lane = lanes((16, NY))
    window = (strip_lane >= HALO) & (strip_lane < 3 * HALO)

    def strips(out, at, start):
        out[at : at + LP] = levels_outer
        out[at + LP : at + LP + 16] = own[start : start + 16]
        out[at + LP + 16 : at + LP + 32] = own_c[start : start + 16]
        out[at + LP + 32 : at + LP + 48] = jnp.where(
            window, roll(outer_c[start : start + 16], 24, 1), outer_r[start : start + 16]
        )

    for m in range(3):
        down[m * LP : (m + 1) * LP] = edge_rows[m]
    strips(down, 3 * LP, NX - 16)
    for m in range(2):
        up[m * LP : (m + 1) * LP] = edge_rows[3 + m]
    strips(up, 2 * LP, 0)


def basis_kernel(
    from_up, from_down, down, up, rhs, coupled, outer, weights,
    basis, dots, correction, rhs_out, parts,
):
    i = lax.axis_index("tx")
    has_up = jnp.where(i > 0, 1.0, 0.0)
    has_down = jnp.where(i < lax.axis_size("tx") - 1, 1.0, 0.0)
    w = weights[0:LP]
    lane16 = lanes((16, NY))
    rim16 = (lane16 < HALO) | (lane16 >= NY - HALO)

    def unpack(ref, count, m):
        return roll(ref[count * LP : (count + 1) * LP], -24 * m, 1)

    def strip(ref, count, has):
        at = (count + 1) * LP
        packed = ref[at + 32 : at + 48]
        return (
            (ref[at : at + 16] * has, jnp.where(rim16, packed, 0.0) * has),
            (ref[at + 16 : at + 32] * has, jnp.where(rim16, roll(packed, -24, 1), 0.0) * has),
        )

    up_r, up_c = strip(from_up, 3, has_up)
    down_r, down_c = strip(from_down, 2, has_down)
    own_r = [rhs[...], outer[0:64]]
    own_c = [coupled[...], outer[64:128]]

    def wet_of(value):
        return jnp.where(value > 0.0, 1.0, 0.0)

    row64 = rows_of((NX, NY))
    row16 = rows_of((16, NY))
    columns_r, columns_c = [], []
    for g in range(2):
        if g == 0:
            lam_u, half_u, speed_u = (from_up[m * LP : (m + 1) * LP] for m in range(3))
            lam_l, half_l, speed_l = (down[m * LP : (m + 1) * LP] for m in range(3))
            lam_d, half_d = (from_down[m * LP : (m + 1) * LP] for m in range(2))
            lam_f, half_f = (up[m * LP : (m + 1) * LP] for m in range(2))
        else:
            lam_u, half_u, speed_u = (unpack(from_up, 3, m) for m in range(3))
            lam_l, half_l, speed_l = (unpack(down, 3, m) for m in range(3))
            lam_d, half_d = (unpack(from_down, 2, 3 + m) for m in range(2))
            lam_f, half_f = (unpack(down, 3, 3 + m) for m in range(2))
        mask = wet_of(own_c[g][0:1]) * wet_of(up_c[g][15:16])
        gradient = mask * (lam_u - lam_f)
        both = half_u + half_f
        mine_u = gradient * (both - speed_u)
        theirs_u = -gradient * (both + speed_u)
        mask = wet_of(own_c[g][NX - 1 :]) * wet_of(down_c[g][0:1])
        gradient = mask * (lam_d - lam_l)
        both = half_d + half_l
        mine_d = gradient * (both + speed_l)
        theirs_d = -gradient * (both - speed_l)
        if g == 0:
            correction[0:LP] = mine_u
            correction[LP : 2 * LP] = mine_d

        def total(values):
            return jnp.sum(w * values, axis=0, keepdims=True)

        own = own_r[g]
        own = own + jnp.where(row64 == 0, total(mine_u), 0.0)
        own = own + jnp.where(row64 == NX - 1, total(mine_d), 0.0)
        above = up_r[g] + jnp.where(row16 == 15, total(theirs_u), 0.0)
        below = down_r[g] + jnp.where(row16 == 0, total(theirs_d), 0.0)
        if g == 0:
            rhs_out[...] = own
        else:
            rim = (lanes((NX, NY)) < HALO) | (lanes((NX, NY)) >= NY - HALO)
            own = jnp.where(rim, own, 0.0)
            above = jnp.where(rim16, above, 0.0)
            below = jnp.where(rim16, below, 0.0)
        low = rows_of((8, NY)) < 4

        def extended(middle, before, after):
            mixed = jnp.where(low, after[8:16], before[0:8])
            return jnp.concatenate([middle, after[0:8], mixed, before[8:16]], axis=0)

        columns_r.append(extended(own, above, below))
        columns_c.append(extended(own_c[g], up_c[g], down_c[g]))
    v = jnp.concatenate(columns_r, axis=1)
    c = jnp.concatenate(columns_c, axis=1)
    wet = wet_of(c)
    face_x = wet * roll(wet, -1, 0)
    face_y = wet * roll(wet, -1, 1)
    degree = face_x + roll(face_x, 1, 0) + face_y + roll(face_y, 1, 1)
    diagonal = (c + 4.0 * degree - MID) * (2.0 / HALF)
    face_x = face_x * (-8.0 / HALF)
    face_y = face_y * (-8.0 / HALF)

    def apply(s):
        out = diagonal * s + face_x * roll(s, -1, 0) + roll(face_x * s, 1, 0)
        return out + face_y * roll(s, -1, 1) + roll(face_y * s, 1, 1)

    def dot(n, a, b):
        product = a[:NX, :NY] * b[:NX, :NY]
        part = product[0:8]
        for t in range(1, 8):
            part = part + product[8 * t : 8 * t + 8]
        parts[n : n + 1, :] = jnp.sum(part, axis=0, keepdims=True)

    parts[24:32, :] = jnp.zeros((8, NY), F32)
    before = v
    basis[0] = v[:NX, :NY]
    dot(0, v, v)
    now = 0.5 * apply(v)
    dot(1, before, now)
    for n in range(1, ITERS):
        basis[n] = now[:NX, :NY]
        dot(2 * n, now, now)
        after = apply(now) - before
        dot(2 * n + 1, now, after)
        before, now = now, after
    sums = jnp.sum(parts[...], axis=1, keepdims=True)
    shape = (32, NY)
    line = jnp.sum(jnp.where(lanes(shape) == rows_of(shape), sums, 0.0), axis=0, keepdims=True)
    dots[...] = jnp.broadcast_to(line, dots.shape)


def solve_kernel(
    weight, gathered, basis, stepped, edges_y, edges_x, mask,
    out, surface, flag, scaled,
):
    step = pl.program_id(0)

    @pl.when(step == 0)
    def _():
        line = jnp.sum(gathered[...], axis=0, keepdims=True)
        shape = (32, NY)
        column = jnp.sum(jnp.where(lanes(shape) == rows_of(shape), line, 0.0), axis=1, keepdims=True)
        d = jnp.broadcast_to(column, shape)[0:24]
        d0 = d[0:1]
        d = d / d0
        row = rows_of((24, NY))
        moment = jnp.where((row & 1) == 0, 2.0 * d - 1.0, 2.0 * d - d[1:2])
        moment = jnp.where(row < 2, d, moment)
        largest = jnp.maximum(jnp.max(jnp.abs(moment), axis=0, keepdims=True), 1.0)
        quarter = 0.5 * HALF
        row16 = rows_of((16, NY))
        r, p = moment, moment
        rc = jnp.where(row16 == 0, 1.0, 0.0)
        pc = rc
        xc = jnp.zeros((16, NY), F32)
        rr = jnp.ones((1, NY), F32)
        worst = jnp.ones((1, NY), F32)
        good = jnp.ones((1, NY), F32)
        for n in range(ITERS):
            shifted = jnp.where(row == 0, p[1:2], roll(p, 1, 0)) + roll(p, -1, 0)
            hp = MID * p + quarter * shifted
            alpha = r[n : n + 1] / hp[n : n + 1]
            good = jnp.where(alpha > 0.0, good, 0.0)
            xc = xc + alpha * pc
            if n == ITERS - 1:
                break
            fresh = r - alpha * hp
            lead = -alpha * (quarter * (2.0 if n == 0 else 1.0))
            beta = lead * fresh[n + 1 : n + 2] / r[n : n + 1]
            image = MID * pc + quarter * (
                roll(pc, 1, 0)
                + jnp.where(row16 == 1, pc[0:1], 0.0)
                + jnp.where(row16 == 15, 0.0, roll(pc, -1, 0))
            )
            rc = rc - alpha * image
            pc = rc + beta * pc
            p = fresh + beta * p
            r = fresh
            rr = rr * beta
            good = jnp.where(rr > 0.0, good, 0.0)
            size = jnp.sum(jnp.abs(rc), axis=0, keepdims=True)
            worst = jnp.maximum(worst, size * size / rr)
        good = jnp.where(worst * largest < GUARD, good, 0.0)
        x = jnp.zeros((NX, NY), F32)
        for n in range(ITERS):
            x = x + xc[n : n + 1] * basis[n]
        x = jnp.where(good > 0.0, x, 0.0)
        surface[...] = x
        scaled[...] = mask[...].astype(F32) * x
        flag[...] = jnp.broadcast_to(good, flag.shape).astype(jnp.int32)

    lane = lanes((NX, NY))
    wx = scaled[...]
    for kk in range(LB):
        k = step * LB + kk
        shifted = pltpu.roll(edges_y[...], 111 + 128 - 2 * k, 1)
        value = stepped[kk] - weight[k] * wx
        out[kk] = value + jnp.where((lane == 0) | (lane == NY - 1), shifted, 0.0)
        out[kk, 0:1, :] += edges_x[pl.ds(k, 1), :]
        out[kk, NX - 1 : NX, :] += edges_x[pl.ds(LP + k, 1), :]


def whole(shape):
    return pl.BlockSpec(shape, lambda *_: (0,) * len(shape))


def arrays(*shapes):
    return tuple(jax.ShapeDtypeStruct(s, F32) for s in shapes)


def extended(value, sides):
    for axis, dim in sides:
        size, length = (lax.axis_size(axis), value.shape[dim])
        up = [(i, i + 1) for i in range(size - 1)]
        down = [(j, i) for i, j in up]
        last = lax.slice_in_dim(value, length - 1, length, axis=dim)
        initial = lax.slice_in_dim(value, 0, 1, axis=dim)
        before = lax.ppermute(last, axis, up)
        after = lax.ppermute(initial, axis, down)
        value = jnp.concatenate([before, value, after], axis=dim)
    return value


def iterate(rhs, land_mask, column_weight):
    sides = (("tx", 0), ("ty", 1))
    wet = extended(land_mask.astype(F32), sides)
    mc = wet[1:-1, 1:-1]
    faces = [mc * wet[2:, 1:-1], mc * wet[:-2, 1:-1], mc * wet[1:-1, 2:], mc * wet[1:-1, :-2]]

    def image_of(s):
        p = extended(s, sides)
        total = faces[0] * (s - p[2:, 1:-1]) + faces[1] * (s - p[:-2, 1:-1])
        total = total + faces[2] * (s - p[1:-1, 2:]) + faces[3] * (s - p[1:-1, :-2])
        return column_weight * s + 4.0 * total

    def total_of(value):
        return lax.psum(jnp.sum(value), ("tx", "ty"))

    def body(_, carry):
        x, r, p, rr = carry
        image = image_of(p)
        alpha = rr / total_of(p * image)
        x, r = x + alpha * p, r - alpha * image
        fresh = total_of(r * r)
        return x, r, r + fresh / rr * p, fresh

    start = (jnp.zeros_like(rhs), rhs, rhs, total_of(rhs * rhs))
    return lax.fori_loop(0, ITERS, body, start)[0]


def on_device(
    adjoint_in, state_theta, state_u, state_v, level_scale, land_mask, level_weights, column_weight
):
    steps = LEVELS // LB
    smem = pl.BlockSpec(memory_space=pltpu.SMEM)
    block = pl.BlockSpec((LB, NX, NY), lambda i: (i, 0, 0))
    following = pl.BlockSpec(
        (1, NX, NY), lambda i: (jnp.minimum((i + 1) * LB, LEVELS - 1), 0, 0)
    )
    tile = (NX, NY)
    stepped, sent, edge_rows, rhs, coupled, weights = pl.pallas_call(
        interior_kernel,
        name="interior",
        grid=(steps,),
        in_specs=[smem, smem, block, following, block, following, block, block, whole(tile), whole(tile)],
        out_specs=(
            block, whole((192 + LP, NY)), whole((5, LP, NY)), whole(tile), whole(tile), whole((LP + 8, NY)),
        ),
        out_shape=arrays(
            (LEVELS, NX, NY), (192 + LP, NY), (5, LP, NY), tile, tile, (LP + 8, NY)
        ),
        scratch_shapes=[pltpu.VMEM(tile, F32)],
    )(
        level_scale, level_weights, adjoint_in, adjoint_in, state_theta, state_theta,
        state_u, state_v, land_mask, column_weight,
    )

    def ring(axis):
        n = lax.axis_size(axis)
        return [(i, (i + 1) % n) for i in range(n)], [((i + 1) % n, i) for i in range(n)]

    onward, back = ring("ty")
    from_south = lax.ppermute(sent, "ty", onward)
    from_north = lax.ppermute(sent, "ty", back)
    down, up, rhs, outer, edges_y = pl.pallas_call(
        column_kernel,
        name="columns",
        out_shape=arrays((4 * LP + 48, NY), (3 * LP + 48, NY), tile, (128, NY), tile),
    )(from_south, from_north, sent, edge_rows, rhs, coupled, weights)
    onward, back = ring("tx")
    from_up = lax.ppermute(down, "tx", onward)
    from_down = lax.ppermute(up, "tx", back)
    devices = lax.axis_size("tx") * lax.axis_size("ty")
    basis, dots, edges_x, rhs = pl.pallas_call(
        basis_kernel,
        name="basis",
        out_shape=arrays((ITERS, NX, NY), (devices, NY), (2 * LP, NY), tile),
        scratch_shapes=[pltpu.VMEM((32, NY), F32)],
    )(from_up, from_down, down, up, rhs, coupled, outer, weights)
    gathered = lax.all_to_all(dots, ("tx", "ty"), 0, 0, tiled=True)
    out, surface, flag = pl.pallas_call(
        solve_kernel,
        name="solve",
        grid=(steps,),
        in_specs=[
            smem, whole((devices, NY)), whole((ITERS, NX, NY)), block, whole(tile), whole((2 * LP, NY)), whole(tile),
        ],
        out_specs=(block, whole(tile), whole((8, NY))),
        out_shape=arrays((LEVELS, NX, NY), tile) + (jax.ShapeDtypeStruct((8, NY), jnp.int32),),
        scratch_shapes=[pltpu.VMEM(tile, F32)],
    )(level_weights, gathered, basis, stepped, edges_y, edges_x, land_mask)

    def unsolved(carry):
        return carry[0] == 0

    def slow(carry):
        _, base, _ = carry
        x = iterate(rhs, land_mask, column_weight)
        scaled = land_mask.astype(F32) * x
        return jnp.int32(1), base - level_weights[:, None, None] * scaled[None], x

    _, out, surface = lax.while_loop(unsolved, slow, (flag[0, 0], out, surface))
    return (out, surface)


def solution(mesh):
    field, plane = P(None, "tx", "ty"), P("tx", "ty")
    return jax.shard_map(
        on_device,
        mesh=mesh,
        in_specs=(field, field, field, field, P(), plane, P(), plane),
        out_specs=(field, plane),
        check_vma=False,
    )
```

```python
import jax
import jax.numpy as jnp
from jax import lax
from jax.experimental import pallas as pl
from jax.experimental.pallas import tpu as pltpu
from jax.sharding import PartitionSpec as P

ITERS = 12
LEVELS = 50
LP = 56
NX, NY = 64, 128
LB = 10
HALO = 12
LOW, HIGH = 0.7, 31.0
MID, HALF = 0.5 * (HIGH + LOW), 0.5 * (HIGH - LOW)
GUARD = 1.0e5
F32 = jnp.float32


def lanes(shape):
    return lax.broadcasted_iota(jnp.int32, shape, len(shape) - 1)


def rows_of(shape):
    return lax.broadcasted_iota(jnp.int32, shape, len(shape) - 2)


def roll(x, shift, axis):
    return pltpu.roll(x, shift % x.shape[axis], axis)


def half_kappa(theta, scale):
    return 0.025 * (1.5 + jnp.tanh(theta.astype(F32) * scale))


def interior_kernel(
    scale, weight, lam, lam_next, theta, theta_next, vel_u, vel_v, mask, column,
    stepped, sent, edge_rows, rhs, coupled, weights_out, flux,
):
    step = pl.program_id(0)
    tile = (NX, NY)
    lane, row = lanes(tile), rows_of(tile)
    wet = mask[...].astype(F32)

    @pl.when(step == 0)
    def _():
        sent[...] = jnp.zeros_like(sent)
        edge_rows[...] = jnp.zeros_like(edge_rows)
        rhs[...] = jnp.zeros_like(rhs)
        flux[...] = jnp.zeros_like(flux)
        weights_out[...] = jnp.zeros_like(weights_out)
        coupled[...] = wet * column[...]

    face_x = jnp.where(row == NX - 1, 0.0, wet * roll(wet, -1, 0))
    face_y = jnp.where(lane == NY - 1, 0.0, wet * roll(wet, -1, 1))
    half = half_kappa(theta[0], scale[0, step * LB])
    below = flux[...]
    total = rhs[...]
    for kk in range(LB):
        k = step * LB + kk
        w = weight[k]
        here = lam[kk]
        if kk + 1 < LB:
            above = lam[kk + 1]
            half_above = half_kappa(theta[kk + 1], scale[0, k + 1])
        else:
            above = lam_next[0]
            half_above = half_kappa(theta_next[0], scale[0, jnp.minimum(k + 1, LEVELS - 1)])
        half_u = vel_u[kk].astype(F32) * (0.5 * scale[1, k])
        half_v = vel_v[kk].astype(F32) * (0.5 * scale[2, k])
        dx = face_x * (roll(here, -1, 0) - here)
        sx = half + roll(half, -1, 0)
        dy = face_y * (roll(here, -1, 1) - here)
        sy = half + roll(half, -1, 1)
        vertical = (half + half_above) * (above - here)
        value = here + dx * (sx + half_u) + roll(dx * (half_u - sx), 1, 0)
        value = value + dy * (sy + half_v) + roll(dy * (half_v - sy), 1, 1)
        value = wet * (value + (vertical - below))
        stepped[kk] = value
        total = total + w * value
        at = 16 + 2 * k
        pair = (lane == at) | (lane == at + 1)
        shift = at + 1
        sent[0:64] = jnp.where(pair, pltpu.roll(here, shift, 1), sent[0:64])
        sent[64:128] = jnp.where(pair, pltpu.roll(half, shift, 1), sent[64:128])
        sent[128:192] = jnp.where(lane == at, pltpu.roll(half_v, shift, 1), sent[128:192])
        edge_rows[0, pl.ds(k, 1), :] = here[NX - 1 :]
        edge_rows[1, pl.ds(k, 1), :] = half[NX - 1 :]
        edge_rows[2, pl.ds(k, 1), :] = half_u[NX - 1 :]
        edge_rows[3, pl.ds(k, 1), :] = here[:1]
        edge_rows[4, pl.ds(k, 1), :] = half[:1]
        weights_out[pl.ds(k, 1), :] = jnp.full((1, NY), w, F32)
        lane8 = lanes((8, NY))
        weights_out[LP : LP + 8, :] = jnp.where(
            (lane8 == at) | (lane8 == at + 1), w, weights_out[LP : LP + 8, :]
        )
        below, half = vertical, half_above
    flux[...] = below
    rhs[...] = total

    @pl.when(step == LEVELS // LB - 1)
    def _():
        rim = (lane < HALO) | (lane >= NY - HALO)
        sent[0:64] = jnp.where(rim, total, sent[0:64])
        sent[64:128] = jnp.where(rim, coupled[...], sent[64:128])
        lane_e = lanes((LP, NY))
        packed = jnp.where((lane_e < HALO) | (lane_e >= NY - HALO), edge_rows[0], 0.0)
        for m in range(1, 5):
            inside = (lane_e >= 24 * m - HALO) & (lane_e < 24 * m + HALO)
            packed = jnp.where(inside, roll(edge_rows[m], 24 * m, 1), packed)
        sent[192 : 192 + LP] = packed


def column_kernel(
    from_south, from_north, sent, edge_rows, rhs, coupled, weights,
    down, up, rhs_out, outer, correction,
):
    j = lax.axis_index("ty")
    has_south = jnp.where(j > 0, 1.0, 0.0)
    has_north = jnp.where(j < lax.axis_size("ty") - 1, 1.0, 0.0)
    tile = (NX, NY)
    lane = lanes(tile)
    even = (lane & 1) == 0
    first, last = lane < HALO, lane >= NY - HALO
    south_c = from_south[64:128] * has_south
    north_c = from_north[64:128] * has_north
    outer_c = jnp.where(first, north_c, jnp.where(last, south_c, 0.0))
    outer_r = jnp.where(
        first, from_north[0:64] * has_north, jnp.where(last, from_south[0:64] * has_south, 0.0)
    )
    own_c = coupled[...]
    wet = jnp.where(own_c > 0.0, 1.0, 0.0)
    outer_wet = jnp.where(outer_c > 0.0, 1.0, 0.0)
    mask = jnp.where(
        even, wet[:, NY - 1 :] * outer_wet[:, :1], wet[:, :1] * outer_wet[:, NY - 1 :]
    )
    lam = jnp.where(even, roll(from_north[0:64], -1, 1), roll(from_south[0:64], 1, 1))
    half = jnp.where(even, roll(from_north[64:128], -1, 1), roll(from_south[64:128], 1, 1))
    speed = jnp.where(even, sent[128:192], -roll(from_south[128:192], 1, 1))
    gradient = mask * (lam - sent[0:64])
    both = half + sent[64:128]
    levels = (lane >= 16) & (lane < 16 + 2 * LEVELS)
    mine = jnp.where(levels, gradient * (both + speed), 0.0)
    theirs = jnp.where(levels, gradient * (speed - both), 0.0)
    correction[...] = mine
    w = weights[LP : LP + 1, :]

    def total(values, which):
        return jnp.sum(jnp.where(which, w * values, 0.0), axis=1, keepdims=True)

    odd = jnp.logical_not(even)
    own = rhs[...]
    own = own + jnp.where(lane == NY - 1, total(mine, even), 0.0)
    own = own + jnp.where(lane == 0, total(mine, odd), 0.0)
    outer_r = outer_r + jnp.where(lane == 0, total(theirs, even), 0.0)
    outer_r = outer_r + jnp.where(lane == NY - 1, total(theirs, odd), 0.0)
    rhs_out[...] = own
    outer[0:64] = outer_r
    outer[64:128] = outer_c
    lane_e = lanes((LP, NY))
    north = (lane_e >= 0) & (lane_e < HALO)
    for m in range(1, 5):
        north = north | ((lane_e >= 24 * m) & (lane_e < 24 * m + HALO))
    levels_outer = jnp.where(north, from_north[192 : 192 + LP], from_south[192 : 192 + LP])
    strip_lane = lanes((16, NY))
    window = (strip_lane >= HALO) & (strip_lane < 3 * HALO)

    def strips(out, at, start):
        out[at : at + LP] = levels_outer
        out[at + LP : at + LP + 16] = own[start : start + 16]
        out[at + LP + 16 : at + LP + 32] = own_c[start : start + 16]
        out[at + LP + 32 : at + LP + 48] = jnp.where(
            window, roll(outer_c[start : start + 16], 24, 1), outer_r[start : start + 16]
        )

    for m in range(3):
        down[m * LP : (m + 1) * LP] = edge_rows[m]
    strips(down, 3 * LP, NX - 16)
    for m in range(2):
        up[m * LP : (m + 1) * LP] = edge_rows[3 + m]
    strips(up, 2 * LP, 0)


def basis_kernel(
    from_up, from_down, down, up, rhs, coupled, outer, weights,
    basis, dots, correction, rhs_out, parts,
):
    i = lax.axis_index("tx")
    has_up = jnp.where(i > 0, 1.0, 0.0)
    has_down = jnp.where(i < lax.axis_size("tx") - 1, 1.0, 0.0)
    w = weights[0:LP]
    lane16 = lanes((16, NY))
    rim16 = (lane16 < HALO) | (lane16 >= NY - HALO)

    def unpack(ref, count, m):
        return roll(ref[count * LP : (count + 1) * LP], -24 * m, 1)

    def strip(ref, count, has):
        at = (count + 1) * LP
        packed = ref[at + 32 : at + 48]
        return (
            (ref[at : at + 16] * has, jnp.where(rim16, packed, 0.0) * has),
            (ref[at + 16 : at + 32] * has, jnp.where(rim16, roll(packed, -24, 1), 0.0) * has),
        )

    up_r, up_c = strip(from_up, 3, has_up)
    down_r, down_c = strip(from_down, 2, has_down)
    own_r = [rhs[...], outer[0:64]]
    own_c = [coupled[...], outer[64:128]]

    def wet_of(value):
        return jnp.where(value > 0.0, 1.0, 0.0)

    row64 = rows_of((NX, NY))
    row16 = rows_of((16, NY))
    columns_r, columns_c = [], []
    for g in range(2):
        if g == 0:
            lam_u, half_u, speed_u = (from_up[m * LP : (m + 1) * LP] for m in range(3))
            lam_l, half_l, speed_l = (down[m * LP : (m + 1) * LP] for m in range(3))
            lam_d, half_d = (from_down[m * LP : (m + 1) * LP] for m in range(2))
            lam_f, half_f = (up[m * LP : (m + 1) * LP] for m in range(2))
        else:
            lam_u, half_u, speed_u = (unpack(from_up, 3, m) for m in range(3))
            lam_l, half_l, speed_l = (unpack(down, 3, m) for m in range(3))
            lam_d, half_d = (unpack(from_down, 2, 3 + m) for m in range(2))
            lam_f, half_f = (unpack(down, 3, 3 + m) for m in range(2))
        mask = wet_of(own_c[g][0:1]) * wet_of(up_c[g][15:16])
        gradient = mask * (lam_u - lam_f)
        both = half_u + half_f
        mine_u = gradient * (both - speed_u)
        theirs_u = -gradient * (both + speed_u)
        mask = wet_of(own_c[g][NX - 1 :]) * wet_of(down_c[g][0:1])
        gradient = mask * (lam_d - lam_l)
        both = half_d + half_l
        mine_d = gradient * (both + speed_l)
        theirs_d = -gradient * (both - speed_l)
        if g == 0:
            correction[0:LP] = mine_u
            correction[LP : 2 * LP] = mine_d

        def total(values):
            return jnp.sum(w * values, axis=0, keepdims=True)

        own = own_r[g]
        own = own + jnp.where(row64 == 0, total(mine_u), 0.0)
        own = own + jnp.where(row64 == NX - 1, total(mine_d), 0.0)
        above = up_r[g] + jnp.where(row16 == 15, total(theirs_u), 0.0)
        below = down_r[g] + jnp.where(row16 == 0, total(theirs_d), 0.0)
        if g == 0:
            rhs_out[...] = own
        else:
            rim = (lanes((NX, NY)) < HALO) | (lanes((NX, NY)) >= NY - HALO)
            own = jnp.where(rim, own, 0.0)
            above = jnp.where(rim16, above, 0.0)
            below = jnp.where(rim16, below, 0.0)
        low = rows_of((8, NY)) < 4

        def extended(middle, before, after):
            mixed = jnp.where(low, after[8:16], before[0:8])
            return jnp.concatenate([middle, after[0:8], mixed, before[8:16]], axis=0)

        columns_r.append(extended(own, above, below))
        columns_c.append(extended(own_c[g], up_c[g], down_c[g]))
    v = jnp.concatenate(columns_r, axis=1)
    c = jnp.concatenate(columns_c, axis=1)
    wet = wet_of(c)
    face_x = wet * roll(wet, -1, 0)
    face_y = wet * roll(wet, -1, 1)
    degree = face_x + roll(face_x, 1, 0) + face_y + roll(face_y, 1, 1)
    diagonal = (c + 4.0 * degree - MID) * (2.0 / HALF)
    face_x = face_x * (-8.0 / HALF)
    face_y = face_y * (-8.0 / HALF)

    def apply(s):
        out = diagonal * s + face_x * roll(s, -1, 0) + roll(face_x * s, 1, 0)
        return out + face_y * roll(s, -1, 1) + roll(face_y * s, 1, 1)

    def dot(n, a, b):
        product = a[:NX, :NY] * b[:NX, :NY]
        part = product[0:8]
        for t in range(1, 8):
            part = part + product[8 * t : 8 * t + 8]
        parts[n : n + 1, :] = jnp.sum(part, axis=0, keepdims=True)

    parts[24:32, :] = jnp.zeros((8, NY), F32)
    before = v
    basis[0] = v[:NX, :NY]
    dot(0, v, v)
    now = 0.5 * apply(v)
    dot(1, before, now)
    for n in range(1, ITERS):
        basis[n] = now[:NX, :NY]
        dot(2 * n, now, now)
        after = apply(now) - before
        dot(2 * n + 1, now, after)
        before, now = now, after
    sums = jnp.sum(parts[...], axis=1, keepdims=True)
    shape = (32, NY)
    line = jnp.sum(jnp.where(lanes(shape) == rows_of(shape), sums, 0.0), axis=0, keepdims=True)
    dots[...] = jnp.broadcast_to(line, dots.shape)


def solve_kernel(
    weight, gathered, basis, stepped, edges_y, edges_x, mask,
    out, surface, flag, scaled,
):
    step = pl.program_id(0)

    @pl.when(step == 0)
    def _():
        line = jnp.sum(gathered[...], axis=0, keepdims=True)
        shape = (32, NY)
        column = jnp.sum(jnp.where(lanes(shape) == rows_of(shape), line, 0.0), axis=1, keepdims=True)
        d = jnp.broadcast_to(column, shape)[0:24]
        d0 = d[0:1]
        d = d / d0
        row = rows_of((24, NY))
        moment = jnp.where((row & 1) == 0, 2.0 * d - 1.0, 2.0 * d - d[1:2])
        moment = jnp.where(row < 2, d, moment)
        largest = jnp.maximum(jnp.max(jnp.abs(moment), axis=0, keepdims=True), 1.0)
        quarter = 0.5 * HALF
        row16 = rows_of((16, NY))
        r, p = moment, moment
        rc = jnp.where(row16 == 0, 1.0, 0.0)
        pc = rc
        xc = jnp.zeros((16, NY), F32)
        rr = jnp.ones((1, NY), F32)
        worst = jnp.ones((1, NY), F32)
        good = jnp.ones((1, NY), F32)
        for n in range(ITERS):
            shifted = jnp.where(row == 0, p[1:2], roll(p, 1, 0)) + roll(p, -1, 0)
            hp = MID * p + quarter * shifted
            alpha = r[n : n + 1] / hp[n : n + 1]
            good = jnp.where(alpha > 0.0, good, 0.0)
            xc = xc + alpha * pc
            if n == ITERS - 1:
                break
            fresh = r - alpha * hp
            lead = -alpha * (quarter * (2.0 if n == 0 else 1.0))
            beta = lead * fresh[n + 1 : n + 2] / r[n : n + 1]
            image = MID * pc + quarter * (
                roll(pc, 1, 0)
                + jnp.where(row16 == 1, pc[0:1], 0.0)
                + jnp.where(row16 == 15, 0.0, roll(pc, -1, 0))
            )
            rc = rc - alpha * image
            pc = rc + beta * pc
            p = fresh + beta * p
            r = fresh
            rr = rr * beta
            good = jnp.where(rr > 0.0, good, 0.0)
            size = jnp.sum(jnp.abs(rc), axis=0, keepdims=True)
            worst = jnp.maximum(worst, size * size / rr)
        good = jnp.where(worst * largest < GUARD, good, 0.0)
        x = jnp.zeros((NX, NY), F32)
        for n in range(ITERS):
            x = x + xc[n : n + 1] * basis[n]
        x = jnp.where(good > 0.0, x, 0.0)
        surface[...] = x
        scaled[...] = mask[...].astype(F32) * x
        flag[0] = jnp.min(good).astype(jnp.int32)

    lane = lanes((NX, NY))
    wx = scaled[...]
    for kk in range(LB):
        k = step * LB + kk
        shifted = pltpu.roll(edges_y[...], 111 + 128 - 2 * k, 1)
        value = stepped[kk] - weight[k] * wx
        out[kk] = value + jnp.where((lane == 0) | (lane == NY - 1), shifted, 0.0)
        out[kk, 0:1, :] += edges_x[pl.ds(k, 1), :]
        out[kk, NX - 1 : NX, :] += edges_x[pl.ds(LP + k, 1), :]


def whole(shape):
    return pl.BlockSpec(shape, lambda *_: (0,) * len(shape))


def arrays(*shapes):
    return tuple(jax.ShapeDtypeStruct(s, F32) for s in shapes)


def on_chip(count):
    return [pl.BlockSpec(memory_space=pltpu.VMEM)] * count


def limit(mebibytes):
    return pltpu.CompilerParams(vmem_limit_bytes=mebibytes << 20)


def extended(value, sides):
    for axis, dim in sides:
        size, length = (lax.axis_size(axis), value.shape[dim])
        up = [(i, i + 1) for i in range(size - 1)]
        down = [(j, i) for i, j in up]
        last = lax.slice_in_dim(value, length - 1, length, axis=dim)
        initial = lax.slice_in_dim(value, 0, 1, axis=dim)
        before = lax.ppermute(last, axis, up)
        after = lax.ppermute(initial, axis, down)
        value = jnp.concatenate([before, value, after], axis=dim)
    return value


def iterate(rhs, land_mask, column_weight):
    sides = (("tx", 0), ("ty", 1))
    wet = extended(land_mask.astype(F32), sides)
    mc = wet[1:-1, 1:-1]
    faces = [mc * wet[2:, 1:-1], mc * wet[:-2, 1:-1], mc * wet[1:-1, 2:], mc * wet[1:-1, :-2]]

    def image_of(s):
        p = extended(s, sides)
        total = faces[0] * (s - p[2:, 1:-1]) + faces[1] * (s - p[:-2, 1:-1])
        total = total + faces[2] * (s - p[1:-1, 2:]) + faces[3] * (s - p[1:-1, :-2])
        return column_weight * s + 4.0 * total

    def total_of(value):
        return lax.psum(jnp.sum(value), ("tx", "ty"))

    def body(_, carry):
        x, r, p, rr = carry
        image = image_of(p)
        alpha = rr / total_of(p * image)
        x, r = x + alpha * p, r - alpha * image
        fresh = total_of(r * r)
        return x, r, r + fresh / rr * p, fresh

    start = (jnp.zeros_like(rhs), rhs, rhs, total_of(rhs * rhs))
    return lax.fori_loop(0, ITERS, body, start)[0]


def on_device(
    adjoint_in, state_theta, state_u, state_v, level_scale, land_mask, level_weights, column_weight
):
    steps = LEVELS // LB
    smem = pl.BlockSpec(memory_space=pltpu.SMEM)
    block = pl.BlockSpec((LB, NX, NY), lambda i: (i, 0, 0))
    following = pl.BlockSpec(
        (1, NX, NY), lambda i: (jnp.minimum((i + 1) * LB, LEVELS - 1), 0, 0)
    )
    tile = (NX, NY)
    adjoint_in, state_theta, state_u, state_v = (
        pltpu.with_memory_space_constraint(x, pltpu.HBM)
        for x in (adjoint_in, state_theta, state_u, state_v)
    )
    stepped, sent, edge_rows, rhs, coupled, weights = pl.pallas_call(
        interior_kernel,
        name="interior",
        grid=(steps,),
        in_specs=[smem, smem, block, following, block, following, block, block] + on_chip(2),
        out_specs=[block] + on_chip(5),
        out_shape=arrays(
            (LEVELS, NX, NY), (192 + LP, NY), (5, LP, NY), tile, tile, (LP + 8, NY)
        ),
        scratch_shapes=[pltpu.VMEM(tile, F32)],
        compiler_params=limit(16),
    )(
        level_scale, level_weights, adjoint_in, adjoint_in, state_theta, state_theta,
        state_u, state_v, land_mask, column_weight,
    )

    def ring(axis):
        n = lax.axis_size(axis)
        return [(i, (i + 1) % n) for i in range(n)], [((i + 1) % n, i) for i in range(n)]

    onward, back = ring("ty")
    from_south = lax.ppermute(sent, "ty", onward)
    from_north = lax.ppermute(sent, "ty", back)
    down, up, rhs, outer, edges_y = pl.pallas_call(
        column_kernel,
        name="columns",
        in_specs=on_chip(7),
        out_specs=on_chip(5),
        compiler_params=limit(8),
        out_shape=arrays((4 * LP + 48, NY), (3 * LP + 48, NY), tile, (128, NY), tile),
    )(from_south, from_north, sent, edge_rows, rhs, coupled, weights)
    onward, back = ring("tx")
    from_up = lax.ppermute(down, "tx", onward)
    from_down = lax.ppermute(up, "tx", back)
    devices = lax.axis_size("tx") * lax.axis_size("ty")
    basis, dots, edges_x, rhs = pl.pallas_call(
        basis_kernel,
        name="basis",
        in_specs=on_chip(8),
        out_specs=on_chip(4),
        compiler_params=limit(8),
        out_shape=arrays((ITERS, NX, NY), (devices, NY), (2 * LP, NY), tile),
        scratch_shapes=[pltpu.VMEM((32, NY), F32)],
    )(from_up, from_down, down, up, rhs, coupled, outer, weights)
    gathered = lax.all_to_all(dots, ("tx", "ty"), 0, 0, tiled=True)
    out, surface, flag = pl.pallas_call(
        solve_kernel,
        name="solve",
        grid=(steps,),
        in_specs=[smem] + on_chip(2) + [block] + on_chip(3),
        out_specs=[block] + on_chip(1) + [smem],
        out_shape=(
            pltpu.HBM((LEVELS, NX, NY), F32),
            jax.ShapeDtypeStruct(tile, F32),
            jax.ShapeDtypeStruct((1,), jnp.int32),
        ),
        scratch_shapes=[pltpu.VMEM(tile, F32)],
        compiler_params=limit(8),
    )(level_weights, gathered, basis, stepped, edges_y, edges_x, land_mask)

    def unsolved(carry):
        return carry[0] == 0

    def slow(carry):
        _, base, _ = carry
        x = iterate(rhs, land_mask, column_weight)
        scaled = land_mask.astype(F32) * x
        return jnp.int32(1), base - level_weights[:, None, None] * scaled[None], x

    _, out, surface = lax.while_loop(unsolved, slow, (flag[0], out, surface))
    return (out, surface)


def solution(mesh):
    field, plane = P(None, "tx", "ty"), P("tx", "ty")
    return jax.shard_map(
        on_device,
        mesh=mesh,
        in_specs=(field, field, field, field, P(), plane, P(), plane),
        out_specs=(field, plane),
        check_vma=False,
    )
```

```python
import jax
import jax.numpy as jnp
from jax import lax
from jax.experimental import pallas as pl
from jax.experimental.pallas import tpu as pltpu
from jax.sharding import PartitionSpec as P

ITERS = 12
LEVELS = 50
LP = 56
NX, NY = 64, 128
LB = 10
CHUNKS = LEVELS // LB
HALO = 12
LOW, HIGH = 0.7, 31.0
MID, HALF = 0.5 * (HIGH + LOW), 0.5 * (HIGH - LOW)
GUARD = 1.0e5
F32 = jnp.float32


def lanes(shape):
    return lax.broadcasted_iota(jnp.int32, shape, len(shape) - 1)


def rows_of(shape):
    return lax.broadcasted_iota(jnp.int32, shape, len(shape) - 2)


def roll(x, shift, axis):
    return pltpu.roll(x, shift % x.shape[axis], axis)


def half_kappa(theta, scale):
    return 0.025 * (1.5 + jnp.tanh(theta.astype(F32) * scale))


def interior_kernel(
    scale, weight, lam_hbm, theta_hbm, u_hbm, v_hbm, mask, column,
    stepped, sent, short, edge_rows, rhs, coupled, weights_out,
    lam, theta, vel_u, vel_v, arrived,
):
    def arrival(c, n):
        source, target = ((lam_hbm, lam), (theta_hbm, theta), (u_hbm, vel_u), (v_hbm, vel_v))[n]
        part = pl.ds(c * LB, LB)
        return pltpu.make_async_copy(source.at[part], target.at[part], arrived.at[n, c])

    for c in range(CHUNKS):
        for n in range(4):
            arrival(c, n).start()
    tile = (NX, NY)
    lane, row = lanes(tile), rows_of(tile)
    wet = mask[...].astype(F32)
    sent[...] = jnp.zeros_like(sent)
    edge_rows[...] = jnp.zeros_like(edge_rows)
    weights_out[...] = jnp.zeros_like(weights_out)
    coupled[...] = wet * column[...]
    face_x = jnp.where(row == NX - 1, 0.0, wet * roll(wet, -1, 0))
    face_y = jnp.where(lane == NY - 1, 0.0, wet * roll(wet, -1, 1))
    for n in range(4):
        arrival(0, n).wait()

    def level(k, half, below, total):
        after = jnp.minimum(k + 1, LEVELS - 1)
        w = weight[k]
        here = lam[k]
        above = lam[after]
        half_above = half_kappa(theta[after], scale[0, after])
        half_u = vel_u[k].astype(F32) * (0.5 * scale[1, k])
        half_v = vel_v[k].astype(F32) * (0.5 * scale[2, k])
        dx = face_x * (roll(here, -1, 0) - here)
        sx = half + roll(half, -1, 0)
        dy = face_y * (roll(here, -1, 1) - here)
        sy = half + roll(half, -1, 1)
        vertical = (half + half_above) * (above - here)
        value = here + dx * (sx + half_u) + roll(dx * (half_u - sx), 1, 0)
        value = value + dy * (sy + half_v) + roll(dy * (half_v - sy), 1, 1)
        value = wet * (value + (vertical - below))
        stepped[k] = value
        total = total + w * value
        at = 16 + 2 * k
        pair = (lane == at) | (lane == at + 1)
        shift = at + 1
        sent[0:64] = jnp.where(pair, pltpu.roll(here, shift, 1), sent[0:64])
        sent[64:128] = jnp.where(pair, pltpu.roll(half, shift, 1), sent[64:128])
        sent[128:192] = jnp.where(lane == at, pltpu.roll(half_v, shift, 1), sent[128:192])
        edge_rows[0, pl.ds(k, 1), :] = here[NX - 1 :]
        edge_rows[1, pl.ds(k, 1), :] = half[NX - 1 :]
        edge_rows[2, pl.ds(k, 1), :] = half_u[NX - 1 :]
        edge_rows[3, pl.ds(k, 1), :] = here[:1]
        edge_rows[4, pl.ds(k, 1), :] = half[:1]
        weights_out[pl.ds(k, 1), :] = jnp.full((1, NY), w, F32)
        lane8 = lanes((8, NY))
        weights_out[LP : LP + 8, :] = jnp.where(
            (lane8 == at) | (lane8 == at + 1), w, weights_out[LP : LP + 8, :]
        )
        return half_above, vertical, total

    def chunk(c, carry):
        @pl.when(c + 1 < CHUNKS)
        def _():
            for n in range(4):
                arrival(c + 1, n).wait()

        for kk in range(LB):
            carry = level(c * LB + kk, *carry)
        return carry

    zero = jnp.zeros(tile, F32)
    total = lax.fori_loop(0, CHUNKS, chunk, (half_kappa(theta[0], scale[0, 0]), zero, zero))[2]
    rhs[...] = total
    rim = (lane < HALO) | (lane >= NY - HALO)
    sent[0:64] = jnp.where(rim, total, sent[0:64])
    sent[64:128] = jnp.where(rim, coupled[...], sent[64:128])
    lane_e = lanes((LP, NY))
    packed = jnp.where((lane_e < HALO) | (lane_e >= NY - HALO), edge_rows[0], 0.0)
    for m in range(1, 5):
        inside = (lane_e >= 24 * m - HALO) & (lane_e < 24 * m + HALO)
        packed = jnp.where(inside, roll(edge_rows[m], 24 * m, 1), packed)
    sent[192 : 192 + LP] = packed
    short[0:128] = sent[0:128]
    short[128 : 128 + LP] = packed


def column_kernel(
    from_south, from_north, sent, edge_rows, rhs, coupled, weights,
    down, up, rhs_out, outer, correction,
):
    j = lax.axis_index("ty")
    has_south = jnp.where(j > 0, 1.0, 0.0)
    has_north = jnp.where(j < lax.axis_size("ty") - 1, 1.0, 0.0)
    tile = (NX, NY)
    lane = lanes(tile)
    even = (lane & 1) == 0
    first, last = lane < HALO, lane >= NY - HALO
    south_c = from_south[64:128] * has_south
    north_c = from_north[64:128] * has_north
    outer_c = jnp.where(first, north_c, jnp.where(last, south_c, 0.0))
    outer_r = jnp.where(
        first, from_north[0:64] * has_north, jnp.where(last, from_south[0:64] * has_south, 0.0)
    )
    own_c = coupled[...]
    wet = jnp.where(own_c > 0.0, 1.0, 0.0)
    outer_wet = jnp.where(outer_c > 0.0, 1.0, 0.0)
    mask = jnp.where(
        even, wet[:, NY - 1 :] * outer_wet[:, :1], wet[:, :1] * outer_wet[:, NY - 1 :]
    )
    lam = jnp.where(even, roll(from_north[0:64], -1, 1), roll(from_south[0:64], 1, 1))
    half = jnp.where(even, roll(from_north[64:128], -1, 1), roll(from_south[64:128], 1, 1))
    speed = jnp.where(even, sent[128:192], -roll(from_south[128:192], 1, 1))
    gradient = mask * (lam - sent[0:64])
    both = half + sent[64:128]
    levels = (lane >= 16) & (lane < 16 + 2 * LEVELS)
    mine = jnp.where(levels, gradient * (both + speed), 0.0)
    theirs = jnp.where(levels, gradient * (speed - both), 0.0)
    correction[...] = mine
    w = weights[LP : LP + 1, :]

    def total(values, which):
        return jnp.sum(jnp.where(which, w * values, 0.0), axis=1, keepdims=True)

    odd = jnp.logical_not(even)
    own = rhs[...]
    own = own + jnp.where(lane == NY - 1, total(mine, even), 0.0)
    own = own + jnp.where(lane == 0, total(mine, odd), 0.0)
    outer_r = outer_r + jnp.where(lane == 0, total(theirs, even), 0.0)
    outer_r = outer_r + jnp.where(lane == NY - 1, total(theirs, odd), 0.0)
    rhs_out[...] = own
    outer[0:64] = outer_r
    outer[64:128] = outer_c
    lane_e = lanes((LP, NY))
    north = (lane_e >= 0) & (lane_e < HALO)
    for m in range(1, 5):
        north = north | ((lane_e >= 24 * m) & (lane_e < 24 * m + HALO))
    levels_outer = jnp.where(north, from_north[128 : 128 + LP], from_south[192 : 192 + LP])
    strip_lane = lanes((16, NY))
    window = (strip_lane >= HALO) & (strip_lane < 3 * HALO)

    def strips(out, at, start):
        out[at : at + LP] = levels_outer
        out[at + LP : at + LP + 16] = own[start : start + 16]
        out[at + LP + 16 : at + LP + 32] = own_c[start : start + 16]
        out[at + LP + 32 : at + LP + 48] = jnp.where(
            window, roll(outer_c[start : start + 16], 24, 1), outer_r[start : start + 16]
        )

    for m in range(3):
        down[m * LP : (m + 1) * LP] = edge_rows[m]
    strips(down, 3 * LP, NX - 16)
    for m in range(2):
        up[m * LP : (m + 1) * LP] = edge_rows[3 + m]
    strips(up, 2 * LP, 0)


def basis_kernel(
    from_up, from_down, down, up, rhs, coupled, outer, weights,
    basis, dots, correction, rhs_out, parts,
):
    i = lax.axis_index("tx")
    has_up = jnp.where(i > 0, 1.0, 0.0)
    has_down = jnp.where(i < lax.axis_size("tx") - 1, 1.0, 0.0)
    w = weights[0:LP]
    lane16 = lanes((16, NY))
    rim16 = (lane16 < HALO) | (lane16 >= NY - HALO)

    def unpack(ref, count, m):
        return roll(ref[count * LP : (count + 1) * LP], -24 * m, 1)

    def strip(ref, count, has):
        at = (count + 1) * LP
        packed = ref[at + 32 : at + 48]
        return (
            (ref[at : at + 16] * has, jnp.where(rim16, packed, 0.0) * has),
            (ref[at + 16 : at + 32] * has, jnp.where(rim16, roll(packed, -24, 1), 0.0) * has),
        )

    up_r, up_c = strip(from_up, 3, has_up)
    down_r, down_c = strip(from_down, 2, has_down)
    own_r = [rhs[...], outer[0:64]]
    own_c = [coupled[...], outer[64:128]]

    def wet_of(value):
        return jnp.where(value > 0.0, 1.0, 0.0)

    row64 = rows_of((NX, NY))
    row16 = rows_of((16, NY))
    columns_r, columns_c = [], []
    for g in range(2):
        if g == 0:
            lam_u, half_u, speed_u = (from_up[m * LP : (m + 1) * LP] for m in range(3))
            lam_l, half_l, speed_l = (down[m * LP : (m + 1) * LP] for m in range(3))
            lam_d, half_d = (from_down[m * LP : (m + 1) * LP] for m in range(2))
            lam_f, half_f = (up[m * LP : (m + 1) * LP] for m in range(2))
        else:
            lam_u, half_u, speed_u = (unpack(from_up, 3, m) for m in range(3))
            lam_l, half_l, speed_l = (unpack(down, 3, m) for m in range(3))
            lam_d, half_d = (unpack(from_down, 2, 3 + m) for m in range(2))
            lam_f, half_f = (unpack(down, 3, 3 + m) for m in range(2))
        mask = wet_of(own_c[g][0:1]) * wet_of(up_c[g][15:16])
        gradient = mask * (lam_u - lam_f)
        both = half_u + half_f
        mine_u = gradient * (both - speed_u)
        theirs_u = -gradient * (both + speed_u)
        mask = wet_of(own_c[g][NX - 1 :]) * wet_of(down_c[g][0:1])
        gradient = mask * (lam_d - lam_l)
        both = half_d + half_l
        mine_d = gradient * (both + speed_l)
        theirs_d = -gradient * (both - speed_l)
        if g == 0:
            correction[0:LP] = mine_u
            correction[LP : 2 * LP] = mine_d

        def total(values):
            return jnp.sum(w * values, axis=0, keepdims=True)

        own = own_r[g]
        own = own + jnp.where(row64 == 0, total(mine_u), 0.0)
        own = own + jnp.where(row64 == NX - 1, total(mine_d), 0.0)
        above = up_r[g] + jnp.where(row16 == 15, total(theirs_u), 0.0)
        below = down_r[g] + jnp.where(row16 == 0, total(theirs_d), 0.0)
        if g == 0:
            rhs_out[...] = own
        else:
            rim = (lanes((NX, NY)) < HALO) | (lanes((NX, NY)) >= NY - HALO)
            own = jnp.where(rim, own, 0.0)
            above = jnp.where(rim16, above, 0.0)
            below = jnp.where(rim16, below, 0.0)
        low = rows_of((8, NY)) < 4

        def extended(middle, before, after):
            mixed = jnp.where(low, after[8:16], before[0:8])
            return jnp.concatenate([middle, after[0:8], mixed, before[8:16]], axis=0)

        columns_r.append(extended(own, above, below))
        columns_c.append(extended(own_c[g], up_c[g], down_c[g]))
    v = jnp.concatenate(columns_r, axis=1)
    c = jnp.concatenate(columns_c, axis=1)
    wet = wet_of(c)
    face_x = wet * roll(wet, -1, 0)
    face_y = wet * roll(wet, -1, 1)
    degree = face_x + roll(face_x, 1, 0) + face_y + roll(face_y, 1, 1)
    diagonal = (c + 4.0 * degree - MID) * (2.0 / HALF)
    face_x = face_x * (-8.0 / HALF)
    face_y = face_y * (-8.0 / HALF)

    def apply(s):
        out = diagonal * s + face_x * roll(s, -1, 0) + roll(face_x * s, 1, 0)
        return out + face_y * roll(s, -1, 1) + roll(face_y * s, 1, 1)

    def dot(n, a, b):
        product = a[:NX, :NY] * b[:NX, :NY]
        part = product[0:8]
        for t in range(1, 8):
            part = part + product[8 * t : 8 * t + 8]
        parts[n : n + 1, :] = jnp.sum(part, axis=0, keepdims=True)

    parts[24:32, :] = jnp.zeros((8, NY), F32)
    before = v
    basis[0] = v[:NX, :NY]
    dot(0, v, v)
    now = 0.5 * apply(v)
    dot(1, before, now)
    for n in range(1, ITERS):
        basis[n] = now[:NX, :NY]
        dot(2 * n, now, now)
        after = apply(now) - before
        dot(2 * n + 1, now, after)
        before, now = now, after
    sums = jnp.sum(parts[...], axis=1, keepdims=True)
    shape = (32, NY)
    line = jnp.sum(jnp.where(lanes(shape) == rows_of(shape), sums, 0.0), axis=0, keepdims=True)
    dots[...] = jnp.broadcast_to(line, dots.shape)


def solve_kernel(
    weight, gathered, basis, stepped, edges_y, edges_x, mask,
    out, surface, flag, values, left,
):
    line = jnp.sum(gathered[...], axis=0, keepdims=True)
    shape = (32, NY)
    column = jnp.sum(jnp.where(lanes(shape) == rows_of(shape), line, 0.0), axis=1, keepdims=True)
    d = jnp.broadcast_to(column, shape)[0:24]
    d0 = d[0:1]
    d = d / d0
    row = rows_of((24, NY))
    moment = jnp.where((row & 1) == 0, 2.0 * d - 1.0, 2.0 * d - d[1:2])
    moment = jnp.where(row < 2, d, moment)
    largest = jnp.maximum(jnp.max(jnp.abs(moment), axis=0, keepdims=True), 1.0)
    quarter = 0.5 * HALF
    row16 = rows_of((16, NY))
    r, p = moment, moment
    rc = jnp.where(row16 == 0, 1.0, 0.0)
    pc = rc
    xc = jnp.zeros((16, NY), F32)
    rr = jnp.ones((1, NY), F32)
    worst = jnp.ones((1, NY), F32)
    good = jnp.ones((1, NY), F32)
    for n in range(ITERS):
        shifted = jnp.where(row == 0, p[1:2], roll(p, 1, 0)) + roll(p, -1, 0)
        hp = MID * p + quarter * shifted
        alpha = r[n : n + 1] / hp[n : n + 1]
        good = jnp.where(alpha > 0.0, good, 0.0)
        xc = xc + alpha * pc
        if n == ITERS - 1:
            break
        fresh = r - alpha * hp
        lead = -alpha * (quarter * (2.0 if n == 0 else 1.0))
        beta = lead * fresh[n + 1 : n + 2] / r[n : n + 1]
        image = MID * pc + quarter * (
            roll(pc, 1, 0)
            + jnp.where(row16 == 1, pc[0:1], 0.0)
            + jnp.where(row16 == 15, 0.0, roll(pc, -1, 0))
        )
        rc = rc - alpha * image
        pc = rc + beta * pc
        p = fresh + beta * p
        r = fresh
        rr = rr * beta
        good = jnp.where(rr > 0.0, good, 0.0)
        size = jnp.sum(jnp.abs(rc), axis=0, keepdims=True)
        worst = jnp.maximum(worst, size * size / rr)
    good = jnp.where(worst * largest < GUARD, good, 0.0)
    x = jnp.zeros((NX, NY), F32)
    for n in range(ITERS):
        x = x + xc[n : n + 1] * basis[n]
    x = jnp.where(good > 0.0, x, 0.0)
    surface[...] = x
    wx = mask[...].astype(F32) * x
    flag[0] = jnp.min(good).astype(jnp.int32)

    lane = lanes((NX, NY))
    rim = (lane == 0) | (lane == NY - 1)

    def departure(c):
        part = pl.ds(c * LB, LB)
        return pltpu.make_async_copy(values.at[part], out.at[part], left.at[c])

    def chunk(c, carry):
        for kk in range(LB):
            k = c * LB + kk
            shifted = pltpu.roll(edges_y[...], 111 + 128 - 2 * k, 1)
            values[k] = stepped[k] - weight[k] * wx + jnp.where(rim, shifted, 0.0)
            values[k, 0:1, :] += edges_x[pl.ds(k, 1), :]
            values[k, NX - 1 : NX, :] += edges_x[pl.ds(LP + k, 1), :]
        departure(c).start()
        return carry

    lax.fori_loop(0, CHUNKS, chunk, 0)
    for c in range(CHUNKS):
        departure(c).wait()


def arrays(*shapes):
    return tuple(jax.ShapeDtypeStruct(s, F32) for s in shapes)


def on_chip(count):
    return [pl.BlockSpec(memory_space=pltpu.VMEM)] * count


def limit(mebibytes):
    return pltpu.CompilerParams(vmem_limit_bytes=mebibytes << 20)


def extended(value, sides):
    for axis, dim in sides:
        size, length = (lax.axis_size(axis), value.shape[dim])
        up = [(i, i + 1) for i in range(size - 1)]
        down = [(j, i) for i, j in up]
        last = lax.slice_in_dim(value, length - 1, length, axis=dim)
        initial = lax.slice_in_dim(value, 0, 1, axis=dim)
        before = lax.ppermute(last, axis, up)
        after = lax.ppermute(initial, axis, down)
        value = jnp.concatenate([before, value, after], axis=dim)
    return value


def iterate(rhs, land_mask, column_weight):
    sides = (("tx", 0), ("ty", 1))
    wet = extended(land_mask.astype(F32), sides)
    mc = wet[1:-1, 1:-1]
    faces = [mc * wet[2:, 1:-1], mc * wet[:-2, 1:-1], mc * wet[1:-1, 2:], mc * wet[1:-1, :-2]]

    def image_of(s):
        p = extended(s, sides)
        total = faces[0] * (s - p[2:, 1:-1]) + faces[1] * (s - p[:-2, 1:-1])
        total = total + faces[2] * (s - p[1:-1, 2:]) + faces[3] * (s - p[1:-1, :-2])
        return column_weight * s + 4.0 * total

    def total_of(value):
        return lax.psum(jnp.sum(value), ("tx", "ty"))

    def body(_, carry):
        x, r, p, rr = carry
        image = image_of(p)
        alpha = rr / total_of(p * image)
        x, r = x + alpha * p, r - alpha * image
        fresh = total_of(r * r)
        return x, r, r + fresh / rr * p, fresh

    start = (jnp.zeros_like(rhs), rhs, rhs, total_of(rhs * rhs))
    return lax.fori_loop(0, ITERS, body, start)[0]


def on_device(
    adjoint_in, state_theta, state_u, state_v, level_scale, land_mask, level_weights, column_weight
):
    smem = pl.BlockSpec(memory_space=pltpu.SMEM)
    hbm = pl.BlockSpec(memory_space=pltpu.HBM)
    tile = (NX, NY)
    adjoint_in, state_theta, state_u, state_v, level_scale, kernel_weights = (
        pltpu.with_memory_space_constraint(x, pltpu.HBM)
        for x in (
            adjoint_in, state_theta, state_u, state_v, level_scale, level_weights
        )
    )
    stepped, sent, short, edge_rows, rhs, coupled, weights = pl.pallas_call(
        interior_kernel,
        name="interior",
        in_specs=[smem] * 2 + [hbm] * 4 + on_chip(2),
        out_specs=on_chip(7),
        out_shape=arrays(
            (LEVELS, NX, NY), (192 + LP, NY), (128 + LP, NY), (5, LP, NY), tile, tile, (LP + 8, NY)
        ),
        scratch_shapes=[
            pltpu.VMEM((LEVELS, NX, NY), F32),
            pltpu.VMEM((LEVELS, NX, NY), jnp.bfloat16),
            pltpu.VMEM((LEVELS, NX, NY), jnp.bfloat16),
            pltpu.VMEM((LEVELS, NX, NY), jnp.bfloat16),
            pltpu.SemaphoreType.DMA((4, CHUNKS)),
        ],
        compiler_params=limit(16),
    )(
        level_scale, kernel_weights, adjoint_in, state_theta,
        state_u, state_v, land_mask, column_weight,
    )

    def ring(axis):
        n = lax.axis_size(axis)
        return [(i, (i + 1) % n) for i in range(n)], [((i + 1) % n, i) for i in range(n)]

    onward, back = ring("ty")
    from_south = lax.ppermute(sent, "ty", onward)
    from_north = lax.ppermute(short, "ty", back)
    down, up, rhs, outer, edges_y = pl.pallas_call(
        column_kernel,
        name="columns",
        in_specs=on_chip(7),
        out_specs=on_chip(5),
        compiler_params=limit(8),
        out_shape=arrays((4 * LP + 48, NY), (3 * LP + 48, NY), tile, (128, NY), tile),
    )(from_south, from_north, sent, edge_rows, rhs, coupled, weights)
    onward, back = ring("tx")
    from_up = lax.ppermute(down, "tx", onward)
    from_down = lax.ppermute(up, "tx", back)
    devices = lax.axis_size("tx") * lax.axis_size("ty")
    basis, dots, edges_x, rhs = pl.pallas_call(
        basis_kernel,
        name="basis",
        in_specs=on_chip(8),
        out_specs=on_chip(4),
        compiler_params=limit(8),
        out_shape=arrays((ITERS, NX, NY), (devices, NY), (2 * LP, NY), tile),
        scratch_shapes=[pltpu.VMEM((32, NY), F32)],
    )(from_up, from_down, down, up, rhs, coupled, outer, weights)
    gathered = lax.all_to_all(dots, ("tx", "ty"), 0, 0, tiled=True)
    out, surface, flag = pl.pallas_call(
        solve_kernel,
        name="solve",
        in_specs=[smem] + on_chip(6),
        out_specs=[hbm] + on_chip(1) + [smem],
        out_shape=(
            pltpu.HBM((LEVELS, NX, NY), F32),
            jax.ShapeDtypeStruct(tile, F32),
            jax.ShapeDtypeStruct((1,), jnp.int32),
        ),
        scratch_shapes=[pltpu.VMEM((LEVELS, NX, NY), F32), pltpu.SemaphoreType.DMA((CHUNKS,))],
        compiler_params=limit(8),
    )(kernel_weights, gathered, basis, stepped, edges_y, edges_x, land_mask)

    def unsolved(carry):
        return carry[0] == 0

    def slow(carry):
        _, base, _ = carry
        x = iterate(rhs, land_mask, column_weight)
        scaled = land_mask.astype(F32) * x
        return jnp.int32(1), base - level_weights[:, None, None] * scaled[None], x

    _, out, surface = lax.while_loop(unsolved, slow, (flag[0], out, surface))
    return (out, surface)


def solution(mesh):
    field, plane = P(None, "tx", "ty"), P("tx", "ty")
    return jax.shard_map(
        on_device,
        mesh=mesh,
        in_specs=(field, field, field, field, P(), plane, P(), plane),
        out_specs=(field, plane),
        check_vma=False,
    )
```

```python
import jax
import jax.numpy as jnp
from jax import lax
from jax.experimental import pallas as pl
from jax.experimental.pallas import tpu as pltpu
from jax.sharding import PartitionSpec as P

ITERS = 12
LEVELS = 50
LP = 56
NX, NY = 64, 128
LB = 10
CHUNKS = LEVELS // LB
HALO = 12
LOW, HIGH = 0.7, 31.0
MID, HALF = 0.5 * (HIGH + LOW), 0.5 * (HIGH - LOW)
GUARD = 1.0e5
F32 = jnp.float32


def lanes(shape):
    return lax.broadcasted_iota(jnp.int32, shape, len(shape) - 1)


def rows_of(shape):
    return lax.broadcasted_iota(jnp.int32, shape, len(shape) - 2)


def roll(x, shift, axis):
    return pltpu.roll(x, shift % x.shape[axis], axis)


def half_kappa(theta, scale):
    return 0.025 * (1.5 + jnp.tanh(theta.astype(F32) * scale))


def interior_kernel(
    scale, weight, lam_hbm, theta_hbm, u_hbm, v_hbm, mask, column,
    stepped, sent, short, edge_rows, rhs, coupled, weights_out,
    lam, theta, vel_u, vel_v, kept, arrived,
):
    def arrival(c, n):
        source, target = ((lam_hbm, lam), (theta_hbm, theta), (u_hbm, vel_u), (v_hbm, vel_v))[n]
        part = pl.ds(c * LB, LB)
        return pltpu.make_async_copy(source.at[part], target.at[part], arrived.at[n, c])

    for c in range(CHUNKS):
        for n in range(4):
            arrival(c, n).start()
    tile = (NX, NY)
    lane, row = lanes(tile), rows_of(tile)
    wet = mask[...].astype(F32)
    sent[...] = jnp.zeros_like(sent)
    edge_rows[...] = jnp.zeros_like(edge_rows)
    weights_out[...] = jnp.zeros_like(weights_out)
    coupled[...] = wet * column[...]
    face_x = jnp.where(row == NX - 1, 0.0, wet * roll(wet, -1, 0))
    face_y = jnp.where(lane == NY - 1, 0.0, wet * roll(wet, -1, 1))
    for n in range(4):
        arrival(0, n).wait()

    def level(k, half, below, total):
        after = jnp.minimum(k + 1, LEVELS - 1)
        w = weight[k]
        here = lam[k]
        above = lam[after]
        half_above = half_kappa(theta[after], scale[0, after])
        half_u = vel_u[k].astype(F32) * (0.5 * scale[1, k])
        half_v = vel_v[k].astype(F32) * (0.5 * scale[2, k])
        dx = face_x * (roll(here, -1, 0) - here)
        sx = half + roll(half, -1, 0)
        dy = face_y * (roll(here, -1, 1) - here)
        sy = half + roll(half, -1, 1)
        vertical = (half + half_above) * (above - here)
        value = here + dx * (sx + half_u) + roll(dx * (half_u - sx), 1, 0)
        value = value + dy * (sy + half_v) + roll(dy * (half_v - sy), 1, 1)
        value = wet * (value + (vertical - below))
        stepped[k] = value
        total = total + w * value
        kept[k] = half
        edge_rows[0, pl.ds(k, 1), :] = here[NX - 1 :]
        edge_rows[1, pl.ds(k, 1), :] = half[NX - 1 :]
        edge_rows[2, pl.ds(k, 1), :] = half_u[NX - 1 :]
        edge_rows[3, pl.ds(k, 1), :] = here[:1]
        edge_rows[4, pl.ds(k, 1), :] = half[:1]
        weights_out[pl.ds(k, 1), :] = jnp.full((1, NY), w, F32)
        return half_above, vertical, total

    def chunk(c, carry):
        @pl.when(c + 1 < CHUNKS)
        def _():
            for n in range(4):
                arrival(c + 1, n).wait()

        for kk in range(LB):
            carry = level(c * LB + kk, *carry)
        return carry

    zero = jnp.zeros(tile, F32)
    total = lax.fori_loop(0, CHUNKS, chunk, (half_kappa(theta[0], scale[0, 0]), zero, zero))[2]
    rhs[...] = total

    def pack(c, packs):
        for kk in range(LB):
            k = c * LB + kk
            at = 16 + 2 * k
            pair = (lane == at) | (lane == at + 1)
            half_v = vel_v[k].astype(F32) * (0.5 * scale[2, k])
            packs = (
                jnp.where(pair, pltpu.roll(lam[k], at + 1, 1), packs[0]),
                jnp.where(pair, pltpu.roll(kept[k], at + 1, 1), packs[1]),
                jnp.where(lane == at, pltpu.roll(half_v, at + 1, 1), packs[2]),
            )
        return packs

    packs = lax.fori_loop(0, CHUNKS, pack, (zero, zero, zero))
    for n in range(3):
        sent[64 * n : 64 * n + 64] = packs[n]
    lane_w, row_w = lanes((LP, NY)), rows_of((LP, NY))
    at_level = (lane_w == 16 + 2 * row_w) | (lane_w == 17 + 2 * row_w)
    weights_out[LP:] = jnp.broadcast_to(
        jnp.sum(jnp.where(at_level, weights_out[0:LP], 0.0), axis=0, keepdims=True), (8, NY)
    )
    rim = (lane < HALO) | (lane >= NY - HALO)
    sent[0:64] = jnp.where(rim, total, sent[0:64])
    sent[64:128] = jnp.where(rim, coupled[...], sent[64:128])
    lane_e = lanes((LP, NY))
    packed = jnp.where((lane_e < HALO) | (lane_e >= NY - HALO), edge_rows[0], 0.0)
    for m in range(1, 5):
        inside = (lane_e >= 24 * m - HALO) & (lane_e < 24 * m + HALO)
        packed = jnp.where(inside, roll(edge_rows[m], 24 * m, 1), packed)
    sent[192 : 192 + LP] = packed
    short[0:128] = sent[0:128]
    short[128 : 128 + LP] = packed


def column_kernel(
    from_south, from_north, sent, edge_rows, rhs, coupled, weights,
    down, up, rhs_out, outer, correction,
):
    j = lax.axis_index("ty")
    has_south = jnp.where(j > 0, 1.0, 0.0)
    has_north = jnp.where(j < lax.axis_size("ty") - 1, 1.0, 0.0)
    tile = (NX, NY)
    lane = lanes(tile)
    even = (lane & 1) == 0
    first, last = lane < HALO, lane >= NY - HALO
    south_c = from_south[64:128] * has_south
    north_c = from_north[64:128] * has_north
    outer_c = jnp.where(first, north_c, jnp.where(last, south_c, 0.0))
    outer_r = jnp.where(
        first, from_north[0:64] * has_north, jnp.where(last, from_south[0:64] * has_south, 0.0)
    )
    own_c = coupled[...]
    wet = jnp.where(own_c > 0.0, 1.0, 0.0)
    outer_wet = jnp.where(outer_c > 0.0, 1.0, 0.0)
    mask = jnp.where(
        even, wet[:, NY - 1 :] * outer_wet[:, :1], wet[:, :1] * outer_wet[:, NY - 1 :]
    )
    lam = jnp.where(even, roll(from_north[0:64], -1, 1), roll(from_south[0:64], 1, 1))
    half = jnp.where(even, roll(from_north[64:128], -1, 1), roll(from_south[64:128], 1, 1))
    speed = jnp.where(even, sent[128:192], -roll(from_south[128:192], 1, 1))
    gradient = mask * (lam - sent[0:64])
    both = half + sent[64:128]
    levels = (lane >= 16) & (lane < 16 + 2 * LEVELS)
    mine = jnp.where(levels, gradient * (both + speed), 0.0)
    theirs = jnp.where(levels, gradient * (speed - both), 0.0)
    correction[...] = mine
    w = weights[LP : LP + 1, :]

    def total(values, which):
        return jnp.sum(jnp.where(which, w * values, 0.0), axis=1, keepdims=True)

    odd = jnp.logical_not(even)
    own = rhs[...]
    own = own + jnp.where(lane == NY - 1, total(mine, even), 0.0)
    own = own + jnp.where(lane == 0, total(mine, odd), 0.0)
    outer_r = outer_r + jnp.where(lane == 0, total(theirs, even), 0.0)
    outer_r = outer_r + jnp.where(lane == NY - 1, total(theirs, odd), 0.0)
    rhs_out[...] = own
    outer[0:64] = outer_r
    outer[64:128] = outer_c
    lane_e = lanes((LP, NY))
    north = (lane_e >= 0) & (lane_e < HALO)
    for m in range(1, 5):
        north = north | ((lane_e >= 24 * m) & (lane_e < 24 * m + HALO))
    levels_outer = jnp.where(north, from_north[128 : 128 + LP], from_south[192 : 192 + LP])
    strip_lane = lanes((16, NY))
    window = (strip_lane >= HALO) & (strip_lane < 3 * HALO)

    def strips(out, at, start):
        out[at : at + LP] = levels_outer
        out[at + LP : at + LP + 16] = own[start : start + 16]
        out[at + LP + 16 : at + LP + 32] = own_c[start : start + 16]
        out[at + LP + 32 : at + LP + 48] = jnp.where(
            window, roll(outer_c[start : start + 16], 24, 1), outer_r[start : start + 16]
        )

    for m in range(3):
        down[m * LP : (m + 1) * LP] = edge_rows[m]
    strips(down, 3 * LP, NX - 16)
    for m in range(2):
        up[m * LP : (m + 1) * LP] = edge_rows[3 + m]
    strips(up, 2 * LP, 0)


def basis_kernel(
    from_up, from_down, down, up, rhs, coupled, outer, weights,
    basis, dots, correction, rhs_out, parts,
):
    i = lax.axis_index("tx")
    has_up = jnp.where(i > 0, 1.0, 0.0)
    has_down = jnp.where(i < lax.axis_size("tx") - 1, 1.0, 0.0)
    w = weights[0:LP]
    lane16 = lanes((16, NY))
    rim16 = (lane16 < HALO) | (lane16 >= NY - HALO)

    def unpack(ref, count, m):
        return roll(ref[count * LP : (count + 1) * LP], -24 * m, 1)

    def strip(ref, count, has):
        at = (count + 1) * LP
        packed = ref[at + 32 : at + 48]
        return (
            (ref[at : at + 16] * has, jnp.where(rim16, packed, 0.0) * has),
            (ref[at + 16 : at + 32] * has, jnp.where(rim16, roll(packed, -24, 1), 0.0) * has),
        )

    up_r, up_c = strip(from_up, 3, has_up)
    down_r, down_c = strip(from_down, 2, has_down)
    own_r = [rhs[...], outer[0:64]]
    own_c = [coupled[...], outer[64:128]]

    def wet_of(value):
        return jnp.where(value > 0.0, 1.0, 0.0)

    row64 = rows_of((NX, NY))
    row16 = rows_of((16, NY))
    columns_r, columns_c = [], []
    for g in range(2):
        if g == 0:
            lam_u, half_u, speed_u = (from_up[m * LP : (m + 1) * LP] for m in range(3))
            lam_l, half_l, speed_l = (down[m * LP : (m + 1) * LP] for m in range(3))
            lam_d, half_d = (from_down[m * LP : (m + 1) * LP] for m in range(2))
            lam_f, half_f = (up[m * LP : (m + 1) * LP] for m in range(2))
        else:
            lam_u, half_u, speed_u = (unpack(from_up, 3, m) for m in range(3))
            lam_l, half_l, speed_l = (unpack(down, 3, m) for m in range(3))
            lam_d, half_d = (unpack(from_down, 2, 3 + m) for m in range(2))
            lam_f, half_f = (unpack(down, 3, 3 + m) for m in range(2))
        mask = wet_of(own_c[g][0:1]) * wet_of(up_c[g][15:16])
        gradient = mask * (lam_u - lam_f)
        both = half_u + half_f
        mine_u = gradient * (both - speed_u)
        theirs_u = -gradient * (both + speed_u)
        mask = wet_of(own_c[g][NX - 1 :]) * wet_of(down_c[g][0:1])
        gradient = mask * (lam_d - lam_l)
        both = half_d + half_l
        mine_d = gradient * (both + speed_l)
        theirs_d = -gradient * (both - speed_l)
        if g == 0:
            correction[0:LP] = mine_u
            correction[LP : 2 * LP] = mine_d

        def total(values):
            return jnp.sum(w * values, axis=0, keepdims=True)

        own = own_r[g]
        own = own + jnp.where(row64 == 0, total(mine_u), 0.0)
        own = own + jnp.where(row64 == NX - 1, total(mine_d), 0.0)
        above = up_r[g] + jnp.where(row16 == 15, total(theirs_u), 0.0)
        below = down_r[g] + jnp.where(row16 == 0, total(theirs_d), 0.0)
        if g == 0:
            rhs_out[...] = own
        else:
            rim = (lanes((NX, NY)) < HALO) | (lanes((NX, NY)) >= NY - HALO)
            own = jnp.where(rim, own, 0.0)
            above = jnp.where(rim16, above, 0.0)
            below = jnp.where(rim16, below, 0.0)
        low = rows_of((8, NY)) < 4

        def extended(middle, before, after):
            mixed = jnp.where(low, after[8:16], before[0:8])
            return jnp.concatenate([middle, after[0:8], mixed, before[8:16]], axis=0)

        columns_r.append(extended(own, above, below))
        columns_c.append(extended(own_c[g], up_c[g], down_c[g]))
    v = jnp.concatenate(columns_r, axis=1)
    c = jnp.concatenate(columns_c, axis=1)
    wet = wet_of(c)
    face_x = wet * roll(wet, -1, 0)
    face_y = wet * roll(wet, -1, 1)
    degree = face_x + roll(face_x, 1, 0) + face_y + roll(face_y, 1, 1)
    diagonal = (c + 4.0 * degree - MID) * (2.0 / HALF)
    face_x = face_x * (-8.0 / HALF)
    face_y = face_y * (-8.0 / HALF)

    def apply(s):
        out = diagonal * s + face_x * roll(s, -1, 0) + roll(face_x * s, 1, 0)
        return out + face_y * roll(s, -1, 1) + roll(face_y * s, 1, 1)

    def dot(n, a, b):
        product = a[:NX, :NY] * b[:NX, :NY]
        part = product[0:8]
        for t in range(1, 8):
            part = part + product[8 * t : 8 * t + 8]
        parts[n : n + 1, :] = jnp.sum(part, axis=0, keepdims=True)

    parts[24:32, :] = jnp.zeros((8, NY), F32)
    before = v
    basis[0] = v[:NX, :NY]
    dot(0, v, v)
    now = 0.5 * apply(v)
    dot(1, before, now)
    for n in range(1, ITERS):
        basis[n] = now[:NX, :NY]
        dot(2 * n, now, now)
        after = apply(now) - before
        dot(2 * n + 1, now, after)
        before, now = now, after
    sums = jnp.sum(parts[...], axis=1, keepdims=True)
    shape = (32, NY)
    line = jnp.sum(jnp.where(lanes(shape) == rows_of(shape), sums, 0.0), axis=0, keepdims=True)
    dots[...] = jnp.broadcast_to(line, dots.shape)


def solve_kernel(
    weight, gathered, basis, stepped, edges_y, edges_x, mask,
    out, surface, flag, values, left,
):
    line = jnp.sum(gathered[...], axis=0, keepdims=True)
    shape = (32, NY)
    column = jnp.sum(jnp.where(lanes(shape) == rows_of(shape), line, 0.0), axis=1, keepdims=True)
    d = jnp.broadcast_to(column, shape)[0:24]
    d0 = d[0:1]
    d = d / d0
    row = rows_of((24, NY))
    moment = jnp.where((row & 1) == 0, 2.0 * d - 1.0, 2.0 * d - d[1:2])
    moment = jnp.where(row < 2, d, moment)
    largest = jnp.maximum(jnp.max(jnp.abs(moment), axis=0, keepdims=True), 1.0)
    quarter = 0.5 * HALF
    row16 = rows_of((16, NY))
    r, p = moment, moment
    rc = jnp.where(row16 == 0, 1.0, 0.0)
    pc = rc
    xc = jnp.zeros((16, NY), F32)
    rr = jnp.ones((1, NY), F32)
    worst = jnp.ones((1, NY), F32)
    good = jnp.ones((1, NY), F32)
    for n in range(ITERS):
        shifted = jnp.where(row == 0, p[1:2], roll(p, 1, 0)) + roll(p, -1, 0)
        hp = MID * p + quarter * shifted
        alpha = r[n : n + 1] / hp[n : n + 1]
        good = jnp.where(alpha > 0.0, good, 0.0)
        xc = xc + alpha * pc
        if n == ITERS - 1:
            break
        fresh = r - alpha * hp
        lead = -alpha * (quarter * (2.0 if n == 0 else 1.0))
        beta = lead * fresh[n + 1 : n + 2] / r[n : n + 1]
        image = MID * pc + quarter * (
            roll(pc, 1, 0)
            + jnp.where(row16 == 1, pc[0:1], 0.0)
            + jnp.where(row16 == 15, 0.0, roll(pc, -1, 0))
        )
        rc = rc - alpha * image
        pc = rc + beta * pc
        p = fresh + beta * p
        r = fresh
        rr = rr * beta
        good = jnp.where(rr > 0.0, good, 0.0)
        size = jnp.sum(jnp.abs(rc), axis=0, keepdims=True)
        worst = jnp.maximum(worst, size * size / rr)
    good = jnp.where(worst * largest < GUARD, good, 0.0)
    x = jnp.zeros((NX, NY), F32)
    for n in range(ITERS):
        x = x + xc[n : n + 1] * basis[n]
    x = jnp.where(good > 0.0, x, 0.0)
    surface[...] = x
    wx = mask[...].astype(F32) * x
    flag[0] = jnp.min(good).astype(jnp.int32)

    lane = lanes((NX, NY))
    rim = (lane == 0) | (lane == NY - 1)

    def departure(c):
        part = pl.ds(c * LB, LB)
        return pltpu.make_async_copy(values.at[part], out.at[part], left.at[c])

    def chunk(c, carry):
        for kk in range(LB):
            k = c * LB + kk
            shifted = pltpu.roll(edges_y[...], 111 + 128 - 2 * k, 1)
            values[k] = stepped[k] - weight[k] * wx + jnp.where(rim, shifted, 0.0)
            values[k, 0:1, :] += edges_x[pl.ds(k, 1), :]
            values[k, NX - 1 : NX, :] += edges_x[pl.ds(LP + k, 1), :]
        departure(c).start()
        return carry

    lax.fori_loop(0, CHUNKS, chunk, 0)
    for c in range(CHUNKS):
        departure(c).wait()


def arrays(*shapes):
    return tuple(jax.ShapeDtypeStruct(s, F32) for s in shapes)


def on_chip(count):
    return [pl.BlockSpec(memory_space=pltpu.VMEM)] * count


def limit(mebibytes):
    return pltpu.CompilerParams(vmem_limit_bytes=mebibytes << 20)


def extended(value, sides):
    for axis, dim in sides:
        size, length = (lax.axis_size(axis), value.shape[dim])
        up = [(i, i + 1) for i in range(size - 1)]
        down = [(j, i) for i, j in up]
        last = lax.slice_in_dim(value, length - 1, length, axis=dim)
        initial = lax.slice_in_dim(value, 0, 1, axis=dim)
        before = lax.ppermute(last, axis, up)
        after = lax.ppermute(initial, axis, down)
        value = jnp.concatenate([before, value, after], axis=dim)
    return value


def iterate(rhs, land_mask, column_weight):
    sides = (("tx", 0), ("ty", 1))
    wet = extended(land_mask.astype(F32), sides)
    mc = wet[1:-1, 1:-1]
    faces = [mc * wet[2:, 1:-1], mc * wet[:-2, 1:-1], mc * wet[1:-1, 2:], mc * wet[1:-1, :-2]]

    def image_of(s):
        p = extended(s, sides)
        total = faces[0] * (s - p[2:, 1:-1]) + faces[1] * (s - p[:-2, 1:-1])
        total = total + faces[2] * (s - p[1:-1, 2:]) + faces[3] * (s - p[1:-1, :-2])
        return column_weight * s + 4.0 * total

    def total_of(value):
        return lax.psum(jnp.sum(value), ("tx", "ty"))

    def body(_, carry):
        x, r, p, rr = carry
        image = image_of(p)
        alpha = rr / total_of(p * image)
        x, r = x + alpha * p, r - alpha * image
        fresh = total_of(r * r)
        return x, r, r + fresh / rr * p, fresh

    start = (jnp.zeros_like(rhs), rhs, rhs, total_of(rhs * rhs))
    return lax.fori_loop(0, ITERS, body, start)[0]


def on_device(
    adjoint_in, state_theta, state_u, state_v, level_scale, land_mask, level_weights, column_weight
):
    smem = pl.BlockSpec(memory_space=pltpu.SMEM)
    hbm = pl.BlockSpec(memory_space=pltpu.HBM)
    tile = (NX, NY)
    adjoint_in, state_theta, state_u, state_v, level_scale, kernel_weights = (
        pltpu.with_memory_space_constraint(x, pltpu.HBM)
        for x in (
            adjoint_in, state_theta, state_u, state_v, level_scale, level_weights
        )
    )
    stepped, sent, short, edge_rows, rhs, coupled, weights = pl.pallas_call(
        interior_kernel,
        name="interior",
        in_specs=[smem] * 2 + [hbm] * 4 + on_chip(2),
        out_specs=on_chip(7),
        out_shape=arrays(
            (LEVELS, NX, NY), (192 + LP, NY), (128 + LP, NY), (5, LP, NY), tile, tile, (LP + 8, NY)
        ),
        scratch_shapes=[
            pltpu.VMEM((LEVELS, NX, NY), F32),
            pltpu.VMEM((LEVELS, NX, NY), jnp.bfloat16),
            pltpu.VMEM((LEVELS, NX, NY), jnp.bfloat16),
            pltpu.VMEM((LEVELS, NX, NY), jnp.bfloat16),
            pltpu.VMEM((LEVELS, NX, NY), F32),
            pltpu.SemaphoreType.DMA((4, CHUNKS)),
        ],
        compiler_params=limit(16),
    )(
        level_scale, kernel_weights, adjoint_in, state_theta,
        state_u, state_v, land_mask, column_weight,
    )

    def ring(axis):
        n = lax.axis_size(axis)
        return [(i, (i + 1) % n) for i in range(n)], [((i + 1) % n, i) for i in range(n)]

    onward, back = ring("ty")
    from_south = lax.ppermute(sent, "ty", onward)
    from_north = lax.ppermute(short, "ty", back)
    down, up, rhs, outer, edges_y = pl.pallas_call(
        column_kernel,
        name="columns",
        in_specs=on_chip(7),
        out_specs=on_chip(5),
        compiler_params=limit(8),
        out_shape=arrays((4 * LP + 48, NY), (3 * LP + 48, NY), tile, (128, NY), tile),
    )(from_south, from_north, sent, edge_rows, rhs, coupled, weights)
    onward, back = ring("tx")
    from_up = lax.ppermute(down, "tx", onward)
    from_down = lax.ppermute(up, "tx", back)
    devices = lax.axis_size("tx") * lax.axis_size("ty")
    basis, dots, edges_x, rhs = pl.pallas_call(
        basis_kernel,
        name="basis",
        in_specs=on_chip(8),
        out_specs=on_chip(4),
        compiler_params=limit(8),
        out_shape=arrays((ITERS, NX, NY), (devices, NY), (2 * LP, NY), tile),
        scratch_shapes=[pltpu.VMEM((32, NY), F32)],
    )(from_up, from_down, down, up, rhs, coupled, outer, weights)
    gathered = lax.all_to_all(dots, ("tx", "ty"), 0, 0, tiled=True)
    out, surface, flag = pl.pallas_call(
        solve_kernel,
        name="solve",
        in_specs=[smem] + on_chip(6),
        out_specs=[hbm] + on_chip(1) + [smem],
        out_shape=(
            pltpu.HBM((LEVELS, NX, NY), F32),
            jax.ShapeDtypeStruct(tile, F32),
            jax.ShapeDtypeStruct((1,), jnp.int32),
        ),
        scratch_shapes=[pltpu.VMEM((LEVELS, NX, NY), F32), pltpu.SemaphoreType.DMA((CHUNKS,))],
        compiler_params=limit(8),
    )(kernel_weights, gathered, basis, stepped, edges_y, edges_x, land_mask)

    def unsolved(carry):
        return carry[0] == 0

    def slow(carry):
        _, base, _ = carry
        x = iterate(rhs, land_mask, column_weight)
        scaled = land_mask.astype(F32) * x
        return jnp.int32(1), base - level_weights[:, None, None] * scaled[None], x

    _, out, surface = lax.while_loop(unsolved, slow, (flag[0], out, surface))
    return (out, surface)


def solution(mesh):
    field, plane = P(None, "tx", "ty"), P("tx", "ty")
    return jax.shard_map(
        on_device,
        mesh=mesh,
        in_specs=(field, field, field, field, P(), plane, P(), plane),
        out_specs=(field, plane),
        check_vma=False,
    )
```

```python
import jax
import jax.numpy as jnp
from jax import lax
from jax.experimental import pallas as pl
from jax.experimental.pallas import tpu as pltpu
from jax.sharding import PartitionSpec as P

ITERS = 12
LEVELS = 50
LP = 56
NX, NY = 64, 128
LB = 10
CHUNKS = LEVELS // LB
HALO = 12
LOW, HIGH = 0.7, 31.0
MID, HALF = 0.5 * (HIGH + LOW), 0.5 * (HIGH - LOW)
GUARD = 1.0e5
F32 = jnp.float32


def lanes(shape):
    return lax.broadcasted_iota(jnp.int32, shape, len(shape) - 1)


def rows_of(shape):
    return lax.broadcasted_iota(jnp.int32, shape, len(shape) - 2)


def roll(x, shift, axis):
    return pltpu.roll(x, shift % x.shape[axis], axis)


def half_kappa(theta, scale):
    return 0.025 * (1.5 + jnp.tanh(theta.astype(F32) * scale))


def interior_kernel(
    scale, weight, lam_hbm, theta_hbm, u_hbm, v_hbm, mask, column,
    stepped, sent, short, edge_rows, rhs, coupled, weights_out,
    lam, theta, vel_u, vel_v, kept, arrived,
):
    def arrival(c, n):
        source, target = ((lam_hbm, lam), (theta_hbm, theta), (u_hbm, vel_u), (v_hbm, vel_v))[n]
        part = pl.ds(c * LB, LB)
        return pltpu.make_async_copy(source.at[part], target.at[part], arrived.at[n, c])

    for c in range(CHUNKS):
        for n in range(4):
            arrival(c, n).start()
    tile = (NX, NY)
    lane, row = lanes(tile), rows_of(tile)
    wet = mask[...].astype(F32)
    sent[...] = jnp.zeros_like(sent)
    edge_rows[...] = jnp.zeros_like(edge_rows)
    weights_out[...] = jnp.zeros_like(weights_out)
    coupled[...] = wet * column[...]
    face_x = jnp.where(row == NX - 1, 0.0, wet * roll(wet, -1, 0))
    face_y = jnp.where(lane == NY - 1, 0.0, wet * roll(wet, -1, 1))
    for n in range(4):
        arrival(0, n).wait()

    def level(k, half, below, total):
        after = jnp.minimum(k + 1, LEVELS - 1)
        w = weight[k]
        here = lam[k]
        above = lam[after]
        half_above = half_kappa(theta[after], scale[0, after])
        half_u = vel_u[k].astype(F32) * (0.5 * scale[1, k])
        half_v = vel_v[k].astype(F32) * (0.5 * scale[2, k])
        dx = face_x * (roll(here, -1, 0) - here)
        sx = half + roll(half, -1, 0)
        dy = face_y * (roll(here, -1, 1) - here)
        sy = half + roll(half, -1, 1)
        vertical = (half + half_above) * (above - here)
        value = here + dx * (sx + half_u) + roll(dx * (half_u - sx), 1, 0)
        value = value + dy * (sy + half_v) + roll(dy * (half_v - sy), 1, 1)
        value = wet * (value + (vertical - below))
        stepped[k] = value
        total = total + w * value
        kept[k] = half
        return half_above, vertical, total

    def chunk(c, carry):
        @pl.when(c + 1 < CHUNKS)
        def _():
            for n in range(4):
                arrival(c + 1, n).wait()

        for kk in range(LB):
            carry = level(c * LB + kk, *carry)
        return carry

    zero = jnp.zeros(tile, F32)
    total = lax.fori_loop(0, CHUNKS, chunk, (half_kappa(theta[0], scale[0, 0]), zero, zero))[2]
    rhs[...] = total

    def pack(c, packs):
        for kk in range(LB):
            k = c * LB + kk
            at = 16 + 2 * k
            pair = (lane == at) | (lane == at + 1)
            half_v = vel_v[k].astype(F32) * (0.5 * scale[2, k])
            half_u = vel_u[k].astype(F32) * (0.5 * scale[1, k])
            edge_rows[0, pl.ds(k, 1), :] = lam[k, NX - 1 :]
            edge_rows[1, pl.ds(k, 1), :] = kept[k, NX - 1 :]
            edge_rows[2, pl.ds(k, 1), :] = half_u[NX - 1 :]
            edge_rows[3, pl.ds(k, 1), :] = lam[k, :1]
            edge_rows[4, pl.ds(k, 1), :] = kept[k, :1]
            weights_out[pl.ds(k, 1), :] = jnp.full((1, NY), weight[k], F32)
            packs = (
                jnp.where(pair, pltpu.roll(lam[k], at + 1, 1), packs[0]),
                jnp.where(pair, pltpu.roll(kept[k], at + 1, 1), packs[1]),
                jnp.where(lane == at, pltpu.roll(half_v, at + 1, 1), packs[2]),
            )
        return packs

    packs = lax.fori_loop(0, CHUNKS, pack, (zero, zero, zero))
    for n in range(3):
        sent[64 * n : 64 * n + 64] = packs[n]
    lane_w, row_w = lanes((LP, NY)), rows_of((LP, NY))
    at_level = (lane_w == 16 + 2 * row_w) | (lane_w == 17 + 2 * row_w)
    weights_out[LP:] = jnp.broadcast_to(
        jnp.sum(jnp.where(at_level, weights_out[0:LP], 0.0), axis=0, keepdims=True), (8, NY)
    )
    rim = (lane < HALO) | (lane >= NY - HALO)
    sent[0:64] = jnp.where(rim, total, sent[0:64])
    sent[64:128] = jnp.where(rim, coupled[...], sent[64:128])
    lane_e = lanes((LP, NY))
    packed = jnp.where((lane_e < HALO) | (lane_e >= NY - HALO), edge_rows[0], 0.0)
    for m in range(1, 5):
        inside = (lane_e >= 24 * m - HALO) & (lane_e < 24 * m + HALO)
        packed = jnp.where(inside, roll(edge_rows[m], 24 * m, 1), packed)
    sent[192 : 192 + LP] = packed
    short[0:128] = sent[0:128]
    short[128 : 128 + LP] = packed


def column_kernel(
    from_south, from_north, sent, edge_rows, rhs, coupled, weights,
    down, up, rhs_out, outer, correction,
):
    j = lax.axis_index("ty")
    has_south = jnp.where(j > 0, 1.0, 0.0)
    has_north = jnp.where(j < lax.axis_size("ty") - 1, 1.0, 0.0)
    tile = (NX, NY)
    lane = lanes(tile)
    even = (lane & 1) == 0
    first, last = lane < HALO, lane >= NY - HALO
    south_c = from_south[64:128] * has_south
    north_c = from_north[64:128] * has_north
    outer_c = jnp.where(first, north_c, jnp.where(last, south_c, 0.0))
    outer_r = jnp.where(
        first, from_north[0:64] * has_north, jnp.where(last, from_south[0:64] * has_south, 0.0)
    )
    own_c = coupled[...]
    wet = jnp.where(own_c > 0.0, 1.0, 0.0)
    outer_wet = jnp.where(outer_c > 0.0, 1.0, 0.0)
    mask = jnp.where(
        even, wet[:, NY - 1 :] * outer_wet[:, :1], wet[:, :1] * outer_wet[:, NY - 1 :]
    )
    lam = jnp.where(even, roll(from_north[0:64], -1, 1), roll(from_south[0:64], 1, 1))
    half = jnp.where(even, roll(from_north[64:128], -1, 1), roll(from_south[64:128], 1, 1))
    speed = jnp.where(even, sent[128:192], -roll(from_south[128:192], 1, 1))
    gradient = mask * (lam - sent[0:64])
    both = half + sent[64:128]
    levels = (lane >= 16) & (lane < 16 + 2 * LEVELS)
    mine = jnp.where(levels, gradient * (both + speed), 0.0)
    theirs = jnp.where(levels, gradient * (speed - both), 0.0)
    correction[...] = mine
    w = weights[LP : LP + 1, :]

    def total(values, which):
        return jnp.sum(jnp.where(which, w * values, 0.0), axis=1, keepdims=True)

    odd = jnp.logical_not(even)
    own = rhs[...]
    own = own + jnp.where(lane == NY - 1, total(mine, even), 0.0)
    own = own + jnp.where(lane == 0, total(mine, odd), 0.0)
    outer_r = outer_r + jnp.where(lane == 0, total(theirs, even), 0.0)
    outer_r = outer_r + jnp.where(lane == NY - 1, total(theirs, odd), 0.0)
    rhs_out[...] = own
    outer[0:64] = outer_r
    outer[64:128] = outer_c
    lane_e = lanes((LP, NY))
    north = (lane_e >= 0) & (lane_e < HALO)
    for m in range(1, 5):
        north = north | ((lane_e >= 24 * m) & (lane_e < 24 * m + HALO))
    levels_outer = jnp.where(north, from_north[128 : 128 + LP], from_south[192 : 192 + LP])
    strip_lane = lanes((16, NY))
    window = (strip_lane >= HALO) & (strip_lane < 3 * HALO)

    def strips(out, at, start):
        out[at : at + LP] = levels_outer
        out[at + LP : at + LP + 16] = own[start : start + 16]
        out[at + LP + 16 : at + LP + 32] = own_c[start : start + 16]
        out[at + LP + 32 : at + LP + 48] = jnp.where(
            window, roll(outer_c[start : start + 16], 24, 1), outer_r[start : start + 16]
        )

    for m in range(3):
        down[m * LP : (m + 1) * LP] = edge_rows[m]
    strips(down, 3 * LP, NX - 16)
    for m in range(2):
        up[m * LP : (m + 1) * LP] = edge_rows[3 + m]
    strips(up, 2 * LP, 0)


def basis_kernel(
    from_up, from_down, down, up, rhs, coupled, outer, weights,
    basis, dots, correction, rhs_out, parts,
):
    i = lax.axis_index("tx")
    has_up = jnp.where(i > 0, 1.0, 0.0)
    has_down = jnp.where(i < lax.axis_size("tx") - 1, 1.0, 0.0)
    w = weights[0:LP]
    lane16 = lanes((16, NY))
    rim16 = (lane16 < HALO) | (lane16 >= NY - HALO)

    def unpack(ref, count, m):
        return roll(ref[count * LP : (count + 1) * LP], -24 * m, 1)

    def strip(ref, count, has):
        at = (count + 1) * LP
        packed = ref[at + 32 : at + 48]
        return (
            (ref[at : at + 16] * has, jnp.where(rim16, packed, 0.0) * has),
            (ref[at + 16 : at + 32] * has, jnp.where(rim16, roll(packed, -24, 1), 0.0) * has),
        )

    up_r, up_c = strip(from_up, 3, has_up)
    down_r, down_c = strip(from_down, 2, has_down)
    own_r = [rhs[...], outer[0:64]]
    own_c = [coupled[...], outer[64:128]]

    def wet_of(value):
        return jnp.where(value > 0.0, 1.0, 0.0)

    row64 = rows_of((NX, NY))
    row16 = rows_of((16, NY))
    columns_r, columns_c = [], []
    for g in range(2):
        if g == 0:
            lam_u, half_u, speed_u = (from_up[m * LP : (m + 1) * LP] for m in range(3))
            lam_l, half_l, speed_l = (down[m * LP : (m + 1) * LP] for m in range(3))
            lam_d, half_d = (from_down[m * LP : (m + 1) * LP] for m in range(2))
            lam_f, half_f = (up[m * LP : (m + 1) * LP] for m in range(2))
        else:
            lam_u, half_u, speed_u = (unpack(from_up, 3, m) for m in range(3))
            lam_l, half_l, speed_l = (unpack(down, 3, m) for m in range(3))
            lam_d, half_d = (unpack(from_down, 2, 3 + m) for m in range(2))
            lam_f, half_f = (unpack(down, 3, 3 + m) for m in range(2))
        mask = wet_of(own_c[g][0:1]) * wet_of(up_c[g][15:16])
        gradient = mask * (lam_u - lam_f)
        both = half_u + half_f
        mine_u = gradient * (both - speed_u)
        theirs_u = -gradient * (both + speed_u)
        mask = wet_of(own_c[g][NX - 1 :]) * wet_of(down_c[g][0:1])
        gradient = mask * (lam_d - lam_l)
        both = half_d + half_l
        mine_d = gradient * (both + speed_l)
        theirs_d = -gradient * (both - speed_l)
        if g == 0:
            correction[0:LP] = mine_u
            correction[LP : 2 * LP] = mine_d

        def total(values):
            return jnp.sum(w * values, axis=0, keepdims=True)

        own = own_r[g]
        own = own + jnp.where(row64 == 0, total(mine_u), 0.0)
        own = own + jnp.where(row64 == NX - 1, total(mine_d), 0.0)
        above = up_r[g] + jnp.where(row16 == 15, total(theirs_u), 0.0)
        below = down_r[g] + jnp.where(row16 == 0, total(theirs_d), 0.0)
        if g == 0:
            rhs_out[...] = own
        else:
            rim = (lanes((NX, NY)) < HALO) | (lanes((NX, NY)) >= NY - HALO)
            own = jnp.where(rim, own, 0.0)
            above = jnp.where(rim16, above, 0.0)
            below = jnp.where(rim16, below, 0.0)
        low = rows_of((8, NY)) < 4

        def extended(middle, before, after):
            mixed = jnp.where(low, after[8:16], before[0:8])
            return jnp.concatenate([middle, after[0:8], mixed, before[8:16]], axis=0)

        columns_r.append(extended(own, above, below))
        columns_c.append(extended(own_c[g], up_c[g], down_c[g]))
    v = jnp.concatenate(columns_r, axis=1)
    c = jnp.concatenate(columns_c, axis=1)
    wet = wet_of(c)
    face_x = wet * roll(wet, -1, 0)
    face_y = wet * roll(wet, -1, 1)
    degree = face_x + roll(face_x, 1, 0) + face_y + roll(face_y, 1, 1)
    diagonal = (c + 4.0 * degree - MID) * (2.0 / HALF)
    face_x = face_x * (-8.0 / HALF)
    face_y = face_y * (-8.0 / HALF)

    def apply(s):
        out = diagonal * s + face_x * roll(s, -1, 0) + roll(face_x * s, 1, 0)
        return out + face_y * roll(s, -1, 1) + roll(face_y * s, 1, 1)

    def dot(n, a, b):
        product = a[:NX, :NY] * b[:NX, :NY]
        part = product[0:8]
        for t in range(1, 8):
            part = part + product[8 * t : 8 * t + 8]
        parts[n : n + 1, :] = jnp.sum(part, axis=0, keepdims=True)

    parts[24:32, :] = jnp.zeros((8, NY), F32)
    before = v
    basis[0] = v[:NX, :NY]
    dot(0, v, v)
    now = 0.5 * apply(v)
    dot(1, before, now)
    for n in range(1, ITERS):
        basis[n] = now[:NX, :NY]
        dot(2 * n, now, now)
        after = apply(now) - before
        dot(2 * n + 1, now, after)
        before, now = now, after
    sums = jnp.sum(parts[...], axis=1, keepdims=True)
    shape = (32, NY)
    line = jnp.sum(jnp.where(lanes(shape) == rows_of(shape), sums, 0.0), axis=0, keepdims=True)
    dots[...] = jnp.broadcast_to(line, dots.shape)


def solve_kernel(
    weight, gathered, basis, stepped, edges_y, edges_x, mask,
    out, surface, flag, values, left,
):
    line = jnp.sum(gathered[...], axis=0, keepdims=True)
    shape = (32, NY)
    column = jnp.sum(jnp.where(lanes(shape) == rows_of(shape), line, 0.0), axis=1, keepdims=True)
    d = jnp.broadcast_to(column, shape)[0:24]
    d0 = d[0:1]
    d = d / d0
    row = rows_of((24, NY))
    moment = jnp.where((row & 1) == 0, 2.0 * d - 1.0, 2.0 * d - d[1:2])
    moment = jnp.where(row < 2, d, moment)
    largest = jnp.maximum(jnp.max(jnp.abs(moment), axis=0, keepdims=True), 1.0)
    quarter = 0.5 * HALF
    row16 = rows_of((16, NY))
    r, p = moment, moment
    rc = jnp.where(row16 == 0, 1.0, 0.0)
    pc = rc
    xc = jnp.zeros((16, NY), F32)
    rr = jnp.ones((1, NY), F32)
    worst = jnp.ones((1, NY), F32)
    good = jnp.ones((1, NY), F32)
    for n in range(ITERS):
        shifted = jnp.where(row == 0, p[1:2], roll(p, 1, 0)) + roll(p, -1, 0)
        hp = MID * p + quarter * shifted
        alpha = r[n : n + 1] / hp[n : n + 1]
        good = jnp.where(alpha > 0.0, good, 0.0)
        xc = xc + alpha * pc
        if n == ITERS - 1:
            break
        fresh = r - alpha * hp
        lead = -alpha * (quarter * (2.0 if n == 0 else 1.0))
        beta = lead * fresh[n + 1 : n + 2] / r[n : n + 1]
        image = MID * pc + quarter * (
            roll(pc, 1, 0)
            + jnp.where(row16 == 1, pc[0:1], 0.0)
            + jnp.where(row16 == 15, 0.0, roll(pc, -1, 0))
        )
        rc = rc - alpha * image
        pc = rc + beta * pc
        p = fresh + beta * p
        r = fresh
        rr = rr * beta
        good = jnp.where(rr > 0.0, good, 0.0)
        size = jnp.sum(jnp.abs(rc), axis=0, keepdims=True)
        worst = jnp.maximum(worst, size * size / rr)
    good = jnp.where(worst * largest < GUARD, good, 0.0)
    x = jnp.zeros((NX, NY), F32)
    for n in range(ITERS):
        x = x + xc[n : n + 1] * basis[n]
    x = jnp.where(good > 0.0, x, 0.0)
    surface[...] = x
    wx = mask[...].astype(F32) * x
    flag[0] = jnp.min(good).astype(jnp.int32)

    lane = lanes((NX, NY))
    rim = (lane == 0) | (lane == NY - 1)

    def departure(c):
        part = pl.ds(c * LB, LB)
        return pltpu.make_async_copy(values.at[part], out.at[part], left.at[c])

    def chunk(c, carry):
        for kk in range(LB):
            k = c * LB + kk
            shifted = pltpu.roll(edges_y[...], 111 + 128 - 2 * k, 1)
            values[k] = stepped[k] - weight[k] * wx + jnp.where(rim, shifted, 0.0)
            values[k, 0:1, :] += edges_x[pl.ds(k, 1), :]
            values[k, NX - 1 : NX, :] += edges_x[pl.ds(LP + k, 1), :]
        departure(c).start()
        return carry

    lax.fori_loop(0, CHUNKS, chunk, 0)
    for c in range(CHUNKS):
        departure(c).wait()


def arrays(*shapes):
    return tuple(jax.ShapeDtypeStruct(s, F32) for s in shapes)


def on_chip(count):
    return [pl.BlockSpec(memory_space=pltpu.VMEM)] * count


def limit(mebibytes):
    return pltpu.CompilerParams(vmem_limit_bytes=mebibytes << 20)


def extended(value, sides):
    for axis, dim in sides:
        size, length = (lax.axis_size(axis), value.shape[dim])
        up = [(i, i + 1) for i in range(size - 1)]
        down = [(j, i) for i, j in up]
        last = lax.slice_in_dim(value, length - 1, length, axis=dim)
        initial = lax.slice_in_dim(value, 0, 1, axis=dim)
        before = lax.ppermute(last, axis, up)
        after = lax.ppermute(initial, axis, down)
        value = jnp.concatenate([before, value, after], axis=dim)
    return value


def iterate(rhs, land_mask, column_weight):
    sides = (("tx", 0), ("ty", 1))
    wet = extended(land_mask.astype(F32), sides)
    mc = wet[1:-1, 1:-1]
    faces = [mc * wet[2:, 1:-1], mc * wet[:-2, 1:-1], mc * wet[1:-1, 2:], mc * wet[1:-1, :-2]]

    def image_of(s):
        p = extended(s, sides)
        total = faces[0] * (s - p[2:, 1:-1]) + faces[1] * (s - p[:-2, 1:-1])
        total = total + faces[2] * (s - p[1:-1, 2:]) + faces[3] * (s - p[1:-1, :-2])
        return column_weight * s + 4.0 * total

    def total_of(value):
        return lax.psum(jnp.sum(value), ("tx", "ty"))

    def body(_, carry):
        x, r, p, rr = carry
        image = image_of(p)
        alpha = rr / total_of(p * image)
        x, r = x + alpha * p, r - alpha * image
        fresh = total_of(r * r)
        return x, r, r + fresh / rr * p, fresh

    start = (jnp.zeros_like(rhs), rhs, rhs, total_of(rhs * rhs))
    return lax.fori_loop(0, ITERS, body, start)[0]


def on_device(
    adjoint_in, state_theta, state_u, state_v, level_scale, land_mask, level_weights, column_weight
):
    smem = pl.BlockSpec(memory_space=pltpu.SMEM)
    hbm = pl.BlockSpec(memory_space=pltpu.HBM)
    tile = (NX, NY)
    adjoint_in, state_theta, state_u, state_v, level_scale, kernel_weights = (
        pltpu.with_memory_space_constraint(x, pltpu.HBM)
        for x in (
            adjoint_in, state_theta, state_u, state_v, level_scale, level_weights
        )
    )
    stepped, sent, short, edge_rows, rhs, coupled, weights = pl.pallas_call(
        interior_kernel,
        name="interior",
        in_specs=[smem] * 2 + [hbm] * 4 + on_chip(2),
        out_specs=on_chip(7),
        out_shape=arrays(
            (LEVELS, NX, NY), (192 + LP, NY), (128 + LP, NY), (5, LP, NY), tile, tile, (LP + 8, NY)
        ),
        scratch_shapes=[
            pltpu.VMEM((LEVELS, NX, NY), F32),
            pltpu.VMEM((LEVELS, NX, NY), jnp.bfloat16),
            pltpu.VMEM((LEVELS, NX, NY), jnp.bfloat16),
            pltpu.VMEM((LEVELS, NX, NY), jnp.bfloat16),
            pltpu.VMEM((LEVELS, NX, NY), F32),
            pltpu.SemaphoreType.DMA((4, CHUNKS)),
        ],
        compiler_params=limit(16),
    )(
        level_scale, kernel_weights, adjoint_in, state_theta,
        state_u, state_v, land_mask, column_weight,
    )

    def ring(axis):
        n = lax.axis_size(axis)
        return [(i, (i + 1) % n) for i in range(n)], [((i + 1) % n, i) for i in range(n)]

    onward, back = ring("ty")
    from_south = lax.ppermute(sent, "ty", onward)
    from_north = lax.ppermute(short, "ty", back)
    down, up, rhs, outer, edges_y = pl.pallas_call(
        column_kernel,
        name="columns",
        in_specs=on_chip(7),
        out_specs=on_chip(5),
        compiler_params=limit(8),
        out_shape=arrays((4 * LP + 48, NY), (3 * LP + 48, NY), tile, (128, NY), tile),
    )(from_south, from_north, sent, edge_rows, rhs, coupled, weights)
    onward, back = ring("tx")
    from_up = lax.ppermute(down, "tx", onward)
    from_down = lax.ppermute(up, "tx", back)
    devices = lax.axis_size("tx") * lax.axis_size("ty")
    basis, dots, edges_x, rhs = pl.pallas_call(
        basis_kernel,
        name="basis",
        in_specs=on_chip(8),
        out_specs=on_chip(4),
        compiler_params=limit(8),
        out_shape=arrays((ITERS, NX, NY), (devices, NY), (2 * LP, NY), tile),
        scratch_shapes=[pltpu.VMEM((32, NY), F32)],
    )(from_up, from_down, down, up, rhs, coupled, outer, weights)
    gathered = lax.all_to_all(dots, ("tx", "ty"), 0, 0, tiled=True)
    out, surface, flag = pl.pallas_call(
        solve_kernel,
        name="solve",
        in_specs=[smem] + on_chip(6),
        out_specs=[hbm] + on_chip(1) + [smem],
        out_shape=(
            pltpu.HBM((LEVELS, NX, NY), F32),
            jax.ShapeDtypeStruct(tile, F32),
            jax.ShapeDtypeStruct((1,), jnp.int32),
        ),
        scratch_shapes=[pltpu.VMEM((LEVELS, NX, NY), F32), pltpu.SemaphoreType.DMA((CHUNKS,))],
        compiler_params=limit(8),
    )(kernel_weights, gathered, basis, stepped, edges_y, edges_x, land_mask)

    def unsolved(carry):
        return carry[0] == 0

    def slow(carry):
        _, base, _ = carry
        x = iterate(rhs, land_mask, column_weight)
        scaled = land_mask.astype(F32) * x
        return jnp.int32(1), base - level_weights[:, None, None] * scaled[None], x

    _, out, surface = lax.while_loop(unsolved, slow, (flag[0], out, surface))
    return (out, surface)


def solution(mesh):
    field, plane = P(None, "tx", "ty"), P("tx", "ty")
    return jax.shard_map(
        on_device,
        mesh=mesh,
        in_specs=(field, field, field, field, P(), plane, P(), plane),
        out_specs=(field, plane),
        check_vma=False,
    )
```
